128 devices in a mesh: seq: 32 (over x, z, core), tp: 4 (over y).
Axes of the slice: x: 4, y: 4, z: 4, core: 2. Of those that a mesh axis runs over, the one named last changes fastest.
Arguments:
- residual: bfloat16 [1024, 2560], P('seq', 'tp'), may hold values from -6 to 6
- queries: bfloat16 [1024, 3072], P('seq', 'tp'), may hold values from -80 to 80
- new_kv: bfloat16 [1024, 512], P('seq'), may hold values from -8 to 8
- cache: bfloat16 [2048, 256, 512], P('seq'), may hold values from -8 to 8
- out_weight: bfloat16 [3072, 2560], P('tp'), may hold values from -0.109375 to 0.109375
- block_counts: int32 [1024], replicated, may hold values from 1 to 8, 2048 in all
- last_fill: int32 [1024], replicated, may hold values from 1 to 256
- block_order: int32 [2048], P('seq'), may hold values from 0 to 2047, each once
Outputs:
- layer_out: bfloat16 [1024, 2560], P('seq', 'tp')
The draws below stay inside these ranges and needn't reach their ends.
Inputs may be any that keep to these rules, and one draw needn't show every extreme that they name: block_counts sums to 2048, and some request has 8 blocks. last_fill of a request is the live tokens of its last block; all its other blocks are full. block_order is a permutation of the pool entries.
All inputs are finite; a program needn't handle non-finite values.
Results may differ from the reference program's by a relative error of at most 0.012.
Values may be sent and summed in bfloat16 or wider, within the bound.
A program may use at most 256 MiB of HBM per device.

```python
import math
import jax
import jax.numpy as jnp
import numpy as np
from jax import lax

D = 2560
HD = 256
HEADS = 12
BLOCK = 256
MAX_BLOCKS = 8
REQUESTS = 1024
BLOCKS = 2048


def draw_queries(key, part):
    noise_key = jax.random.fold_in(key, 11)
    result = jax.random.normal(noise_key, (REQUESTS, HEADS * HD), jnp.float32)
    return jnp.clip(result, -80.0, 80.0).astype(jnp.bfloat16)


def draw_new_kv(key, part):
    noise_key = jax.random.fold_in(key, 13)
    result = jax.random.normal(noise_key, (REQUESTS, 2 * HD), jnp.float32)
    return jnp.clip(result, -8.0, 8.0).astype(jnp.bfloat16)


def draw_cache(key, part):
    noise_key = jax.random.fold_in(key, 17)
    result = jax.random.normal(noise_key, (BLOCKS, BLOCK, 2 * HD), jnp.float32)
    return jnp.clip(result, -8.0, 8.0).astype(jnp.bfloat16)


def with_ends(array, stream_key, low, high):
    index_at = [jax.random.randint(jax.random.fold_in(stream_key, axis), (), 0, length) for axis, length in enumerate(array.shape)]
    longest = array.shape.index(max(array.shape))
    neighbour = index_at[:longest] + [(index_at[longest] + 1) % array.shape[longest]] + index_at[longest + 1:]
    return array.at[tuple(index_at)].set(low).at[tuple(neighbour)].set(high)


def block_levels(stream_key, shape, cuts, smallest, largest):
    level = 1.0
    for position, parts in cuts:
        heights = jax.random.uniform(jax.random.fold_in(jax.random.fold_in(stream_key, 6), position), (parts,), jnp.float32, smallest / len(cuts), largest / len(cuts))
        level = level * jnp.repeat(jnp.exp(heights), shape[position] // parts).reshape((-1,) + (1,) * (len(shape) - 1 - position))
    return level


def profile(number_of, total, most, skew):
    portions = [(1 << 20) // math.isqrt(rank ** skew) + 1 for rank in range(2, number_of + 1)]
    surplus, holding = total - most - (number_of - 1), [1] * (number_of - 1)
    while surplus > 0:
        movable = [i for i in range(number_of - 1) if holding[i] < most]
        pool, remaining = sum([portions[i] for i in movable]), surplus
        for i in movable:
            addition = min(most - holding[i], max(1, remaining * portions[i] // pool), surplus)
            holding[i] = holding[i] + addition
            surplus = surplus - addition
    return np.array([most] + holding)


def uneven(rng, number_of, total, bound, lean):
    if number_of == 2:
        one = jax.random.randint(rng, (), max(1, total - bound), min(bound, total - 1) + 1)
        return jnp.stack([one, total - one])
    lengths = jnp.asarray(profile(number_of, total, bound, lean), jnp.int32)
    pairs = (number_of - 1) // 2
    donor, sink = lengths[1:1 + 2 * pairs:2], lengths[2:2 + 2 * pairs:2]
    slack = jnp.minimum(donor - 1, bound - sink)
    passed = jax.random.randint(jax.random.fold_in(rng, 1), (pairs,), 0, 1 << 20) % (slack + 1)
    lengths = lengths.at[1:1 + 2 * pairs:2].set(donor - passed).at[2:2 + 2 * pairs:2].set(sink + passed)
    return lengths[jax.random.permutation(jax.random.fold_in(rng, 2), number_of)]


def normal_values(stream_key, shape, scale, limit, split=(), kind=jnp.bfloat16):
    values = jax.random.normal(stream_key, shape, jnp.float32) * scale
    if len(split) > 0:
        values = block_levels(stream_key, shape, split, -0.22, 0.18) * values
    return jnp.clip(values, min=-limit, max=limit).astype(kind)


def setup_inputs(seed: int = 0) -> dict:
    streams_of = jax.random.split(jax.random.key(seed), 9)
    return {
        "residual": normal_values(streams_of[0], (REQUESTS, D), 1.0, 6.0, ((0, 32), (1, 4))),
        "queries": draw_queries(jax.random.fold_in(streams_of[8], 71), 0),
        "new_kv": draw_new_kv(jax.random.fold_in(streams_of[8], 71), 0),
        "cache": draw_cache(jax.random.fold_in(streams_of[8], 71), 0),
        "out_weight": normal_values(streams_of[4], (HEADS * HD, D), (HEADS * HD) ** -0.5, 0.109375, ((0, 4),)),
        "block_counts": uneven(streams_of[5], REQUESTS, BLOCKS, MAX_BLOCKS, 2).astype(jnp.int32),
        "last_fill": with_ends(jax.random.randint(streams_of[6], (REQUESTS,), 1, BLOCK + 1), jax.random.fold_in(streams_of[6], 1), 1, BLOCK).astype(jnp.int32),
        "block_order": jax.random.permutation(streams_of[7], BLOCKS).astype(jnp.int32),
    }


very_low = -1e30


def place_blocks(block_counts, block_order):
    num_req = block_counts.shape[0]
    ends = jnp.cumsum(block_counts).astype(jnp.int32)
    pool_start = (ends - block_counts).astype(jnp.int32)
    block_req = (jnp.sum((pool_start[None, :] <= block_order[:, None]).astype(jnp.int32), axis=1) - 1).astype(jnp.int32)
    onehot = block_req[:, None] == jnp.arange(num_req, dtype=jnp.int32)[None, :]
    start_here = jnp.sum(jnp.where(onehot, pool_start[None, :], 0), axis=1).astype(jnp.int32)
    count_here = jnp.sum(jnp.where(onehot, block_counts[None, :], 0), axis=1).astype(jnp.int32)
    return block_req, (block_order - start_here).astype(jnp.int32), count_here, onehot


def reference(residual, queries, new_kv, cache, out_weight, block_counts, last_fill, block_order):
    num_req = residual.shape[0]
    inv_root = 1.0 / (HD ** 0.5)
    block_req, block_slot, count_here, onehot = place_blocks(block_counts, block_order)
    fill_here = jnp.sum(jnp.where(onehot, last_fill[None, :], 0), axis=1)
    live_mask = (block_slot < count_here - 1)[:, None] | (jnp.arange(BLOCK, dtype=jnp.int32)[None, :] < fill_here[:, None])
    query_heads = queries.astype(jnp.float32).reshape(num_req, HEADS, HD)
    keys = cache[:, :, :HD].astype(jnp.float32)
    values = cache[:, :, HD:].astype(jnp.float32)
    query_blocks = query_heads[block_req]
    scores = jnp.einsum('bhd,btd->bht', query_blocks, keys) * inv_root
    scores = jnp.where(live_mask[:, None, :], scores, very_low)
    block_max = jnp.max(scores, axis=2)
    weights = jnp.where(live_mask[:, None, :], jnp.exp(scores - block_max[:, :, None]), 0.0)
    block_sum = jnp.sum(weights, axis=2)
    rounded = lax.optimization_barrier(weights.astype(jnp.bfloat16)).astype(jnp.float32)
    block_acc = jnp.einsum('bht,btd->bhd', rounded, values)
    cache_max = jax.ops.segment_max(block_max, block_req, num_segments=num_req)
    factor = jnp.exp(block_max - cache_max[block_req])
    cache_sum = jax.ops.segment_sum(block_sum * factor, block_req, num_segments=num_req)
    cache_acc = jax.ops.segment_sum(block_acc * factor[:, :, None], block_req, num_segments=num_req)
    new_key = new_kv[:, :HD].astype(jnp.float32)
    new_value = new_kv[:, HD:].astype(jnp.float32)
    own_score = jnp.einsum('rhd,rd->rh', query_heads, new_key) * inv_root
    top_score = jnp.maximum(cache_max, own_score)
    cache_factor = jnp.exp(cache_max - top_score)
    own_factor = jnp.exp(own_score - top_score)
    denominator = cache_sum * cache_factor + own_factor
    mixed_sum = cache_acc * cache_factor[:, :, None] + own_factor[:, :, None] * new_value[:, None, :]
    attention = (mixed_sum / denominator[:, :, None]).reshape(num_req, HEADS * HD).astype(jnp.bfloat16)
    projected = jnp.dot(attention, out_weight, preferred_element_type=jnp.float32)
    return (residual.astype(jnp.float32) + projected).astype(jnp.bfloat16)
```

```python
import jax
import jax.numpy as jnp
from jax import lax
from jax.experimental import pallas as pl
from jax.experimental.pallas import tpu as pltpu
from jax.sharding import PartitionSpec as P

MESH = pl.DeviceIdType.MESH
VERY_LOW = -1e30
RING = 4
GROUPS = 4


def kernel(
    order_hbm, counts_hbm, fill_hbm, residual_hbm, queries_hbm, new_kv_hbm, cache_hbm, weight_hbm,
    out_ref,
    cache, weight, residual, new_kv, q_own, counts, fill, order_all, q_all, ends_ref, starts_ref,
    onehot_ref, q_blk, live, o_scr, o_all, lse_all, tab, tab_lse, fwd, fwd_lse, home, home_lse,
    part, part_in, send_sem, recv_sem, cache_sem, local_sem,
):
    num_blocks, block_len, width = cache.shape
    head_dim = width // 2
    rows = q_own.shape[0]
    heads = q_own.shape[1] // head_dim
    cols = residual.shape[1]
    per_group = num_blocks // GROUPS
    inv_root = 1.0 / head_dim**0.5
    f32, bf16 = jnp.float32, jnp.bfloat16

    me = lax.axis_index("seq")
    tp = lax.axis_index("tp")
    core = lax.rem(me, 2)
    other = 1 - core
    chip = lax.div(me, 2)
    x = lax.div(chip, RING)
    z = lax.rem(chip, RING)
    f = x * other + z * core
    s = z * other + x * core

    def seq_of(fi, si, ci):
        xi = fi * other + si * core
        zi = si * other + fi * core
        return (xi * RING + zi) * 2 + ci

    def ring(a, k):
        return lax.rem(a + k + RING, RING)

    f_up = (seq_of(ring(f, 1), s, core), tp)
    f_dn = (seq_of(ring(f, -1), s, core), tp)
    s_up = (seq_of(f, ring(s, 1), core), tp)
    s_dn = (seq_of(f, ring(s, -1), core), tp)
    s_up_x = (seq_of(f, ring(s, 1), other), tp)
    s_dn_x = (seq_of(f, ring(s, -1), other), tp)
    f_up_x = (seq_of(ring(f, 1), s, other), tp)
    f_dn_x = (seq_of(ring(f, -1), s, other), tp)
    sib = (seq_of(f, s, other), tp)
    tps = [(me, lax.rem(tp + k, RING)) for k in range(1, RING)]

    per_copy = num_blocks // 8
    own_q = pltpu.make_async_copy(queries_hbm, q_own, local_sem.at[0])
    own_q.start()
    small = [
        pltpu.make_async_copy(order_hbm, order_all.at[f], local_sem.at[1]),
        pltpu.make_async_copy(counts_hbm, counts, local_sem.at[2]),
        pltpu.make_async_copy(fill_hbm, fill, local_sem.at[3]),
        pltpu.make_async_copy(new_kv_hbm, new_kv, local_sem.at[4]),
        pltpu.make_async_copy(residual_hbm, residual, local_sem.at[5]),
        pltpu.make_async_copy(queries_hbm, q_all.at[me], local_sem.at[6]),
    ]
    for copy in small:
        copy.start()

    barrier = pltpu.get_barrier_semaphore()
    peers = [f_up, f_dn, s_up, s_dn, s_up_x, s_dn_x, f_up_x, f_dn_x, sib] + tps
    for peer in peers:
        pl.semaphore_signal(barrier, inc=1, device_id=peer, device_id_type=MESH)

    cache_copies = [
        pltpu.make_async_copy(
            cache_hbm.at[pl.ds(i * per_copy, per_copy)],
            cache.at[pl.ds(i * per_copy, per_copy)],
            cache_sem.at[i],
        )
        for i in range(8)
    ]
    for copy in cache_copies:
        copy.start()
    weight_copies = [
        pltpu.make_async_copy(
            weight_hbm.at[:, pl.ds(t * cols, cols)], weight.at[t], local_sem.at[7 + t]
        )
        for t in range(RING)
    ]
    for copy in weight_copies:
        copy.start()

    started = []

    def send(src, dst, peer):
        n = len(started)
        copy = pltpu.make_async_remote_copy(
            src_ref=src, dst_ref=dst, send_sem=send_sem.at[n], recv_sem=recv_sem.at[n],
            device_id=peer, device_id_type=MESH,
        )
        copy.start()
        started.append(copy)
        return copy

    own_q.wait()
    pl.semaphore_wait(barrier, len(peers))

    half = rows // 2
    top, bottom = pl.ds(0, half), pl.ds(half, half)

    def chunk(i, j):
        return q_all.at[seq_of(ring(f, i), ring(s, j), core)]

    def part_of(i, j, which):
        return q_all.at[seq_of(ring(f, i), ring(s, j), core), which]

    sib_copies = []

    def to_sib(i, j, src=None):
        c = chunk(i, j)
        sib_copies.append(send(c if src is None else src, c, sib))

    def to_s(i, src=None):
        c = chunk(i, 0)
        return (send(c if src is None else src, c, s_up), send(c if src is None else src, c, s_dn))

    own_up = send(q_own, chunk(0, 0), f_up)
    own_dn = send(q_own, chunk(0, 0), f_dn)
    s_copies = {0: to_s(0, q_own)}
    order_own = order_all.at[f]
    to_sib(0, 0, q_own)

    for copy in small:
        copy.wait()
    order_up = send(order_own, order_own, f_up)
    order_dn = send(order_own, order_own, f_dn)

    counts_f = counts[...].astype(f32)
    fill_f = fill[...].astype(f32)
    lane_n = counts_f.shape[1]
    sub_i = lax.broadcasted_iota(jnp.int32, (lane_n, lane_n), 0)
    lane_i = lax.broadcasted_iota(jnp.int32, (lane_n, lane_n), 1)
    upper = (sub_i <= lane_i).astype(f32).astype(bf16)
    cum = jnp.dot(counts_f.astype(bf16), upper, preferred_element_type=f32)
    before = jnp.zeros((1, 1), f32)
    pieces = counts_f.shape[0]
    for k in range(pieces):
        ends_k = cum[k:k + 1, :] + before
        ends_ref[k:k + 1, :] = ends_k
        starts_ref[k:k + 1, :] = ends_k - counts_f[k:k + 1, :]
        before = before + jnp.sum(counts_f[k:k + 1, :], axis=1, keepdims=True)

    sub64 = lax.broadcasted_iota(jnp.int32, (num_blocks, num_blocks), 0)
    lane64 = lax.broadcasted_iota(jnp.int32, (num_blocks, num_blocks), 1)
    order_row = order_all[f].astype(f32)
    order_col = jnp.sum(
        jnp.where(sub64 == lane64, jnp.broadcast_to(order_row, (num_blocks, num_blocks)), 0.0),
        axis=1, keepdims=True,
    )
    fill_raw = jnp.zeros((num_blocks, lane_n), f32)
    for k in range(pieces):
        ends_k = ends_ref[k:k + 1, :]
        starts_k = starts_ref[k:k + 1, :]
        hit = (starts_k <= order_col) & (order_col < ends_k)
        onehot_ref[:, k * lane_n:(k + 1) * lane_n] = jnp.where(hit, 1.0, 0.0).astype(bf16)
        fill_raw = fill_raw + jnp.where(ends_k == order_col + 1.0, fill_f[k:k + 1, :], 0.0)
    fill_sum = jnp.sum(fill_raw, axis=1, keepdims=True)
    live_n = jnp.where(fill_sum > 0.0, fill_sum, float(block_len))
    for h in range(8):
        live[:, h, :] = jnp.broadcast_to(live_n, (num_blocks, block_len))
    q_blk[...] = jnp.zeros(q_blk.shape, f32)

    own_up.wait_recv()
    fwd_up = send(part_of(-1, 0, top), part_of(-1, 0, top), f_up)
    s_copies[-1] = to_s(-1)
    own_dn.wait_recv()
    fwd_dn = send(part_of(1, 0, bottom), part_of(1, 0, bottom), f_dn)
    s_copies[1] = to_s(1)
    to_sib(-1, 0)
    to_sib(1, 0)
    order_up.wait_recv()
    order_dn.wait_recv()
    order_from = order_all.at[ring(f, -1)]
    order_fwd = send(order_from, order_from, f_up)

    s_fwd = {}

    def forward_s(i):
        up, dn = s_copies[i]
        up.wait_recv()
        a = send(part_of(i, -1, top), part_of(i, -1, top), s_up)
        dn.wait_recv()
        b = send(part_of(i, 1, bottom), part_of(i, 1, bottom), s_dn)
        s_fwd[i] = (a, b)
        to_sib(i, -1)
        to_sib(i, 1)

    forward_s(0)
    fwd_up.wait_recv()
    fwd_dn.wait_recv()
    s_copies[2] = to_s(2)
    to_sib(2, 0)
    forward_s(-1)
    forward_s(1)
    for copy in s_fwd[0]:
        copy.wait_recv()
    to_sib(0, 2)
    forward_s(2)
    for i in (-1, 1, 2):
        for copy in s_fwd[i]:
            copy.wait_recv()
        to_sib(i, 2)
    for copy in sib_copies:
        copy.wait_recv()

    picked = jnp.dot(
        onehot_ref[...], q_all[...].reshape(q_all.shape[0] * rows, heads * head_dim),
        preferred_element_type=f32,
    )
    for h in range(heads):
        q_blk[:, h, :] = picked[:, h * head_dim:(h + 1) * head_dim]

    lse_all[f] = jnp.zeros((8, lane_n), f32)
    token = lax.broadcasted_iota(jnp.int32, (8, block_len), 1).astype(f32)
    lane8 = lax.broadcasted_iota(jnp.int32, (8, lane_n), 1)
    o_sends, o_fwds = [], []

    def forward_o(g):
        up, dn = o_sends[g]
        up.wait_recv()
        dn.wait_recv()
        if g % 2 == 0:
            ref = o_all.at[ring(f, -1), g]
            o_fwds.append(send(ref, ref, f_up))
        else:
            ref = o_all.at[ring(f, 1), g]
            o_fwds.append(send(ref, ref, f_dn))

    for g in range(GROUPS):
        for i in range(8 // GROUPS):
            cache_copies[g * (8 // GROUPS) + i].wait()
        blocks = range(g * per_group, (g + 1) * per_group)
        lse_rows = lse_all[f]
        scores = []
        for b in blocks:
            q8 = q_blk[b].astype(bf16)
            scores.append(
                lax.dot_general(
                    q8, cache[b, :, :head_dim], (((1,), (1,)), ((), ())), preferred_element_type=f32
                )
            )
        for b, score in zip(blocks, scores):
            alive = token < live[b]
            score = jnp.where(alive, score * inv_root, VERY_LOW)
            top_b = jnp.max(score, axis=1, keepdims=True)
            w = jnp.where(alive, jnp.exp(score - top_b), 0.0)
            total = jnp.sum(w, axis=1, keepdims=True)
            acc = jnp.dot(w.astype(bf16), cache[b, :, head_dim:], preferred_element_type=f32)
            o_scr[b] = acc / total
            lse_rows = jnp.where(lane8 == b, top_b + jnp.log(total), lse_rows)
        lse_all[f] = lse_rows
        for h in range(heads):
            o_all[f, g, :, h * head_dim:(h + 1) * head_dim] = (
                o_scr[g * per_group:(g + 1) * per_group, h, :].astype(bf16)
            )
        ref = o_all.at[f, g]
        o_sends.append((send(ref, ref, f_up), send(ref, ref, f_dn)))
        if g >= 2:
            forward_o(g - 2)
    ref = lse_all.at[f]
    lse_up, lse_dn = send(ref, ref, f_up), send(ref, ref, f_dn)

    q_f = q_own[...].astype(f32)
    new_key = new_kv[:, :head_dim].astype(f32)
    own_score = [
        jnp.sum(q_f[:, h * head_dim:(h + 1) * head_dim] * new_key, axis=1, keepdims=True) * inv_root
        for h in range(heads)
    ]
    for copy in weight_copies:
        copy.wait()

    forward_o(GROUPS - 2)
    forward_o(GROUPS - 1)
    lse_up.wait_recv()
    lse_dn.wait_recv()
    ref = lse_all.at[ring(f, -1)]
    lse_fwd = send(ref, ref, f_up)
    order_fwd.wait_recv()
    for copy in o_fwds:
        copy.wait_recv()
    lse_fwd.wait_recv()

    def pair(a, b):
        lanes = lax.broadcasted_iota(jnp.int32, a.shape, 1)
        return jnp.where(lanes < num_blocks, a, pltpu.roll(b, num_blocks, 1))

    lse = jnp.concatenate(
        [pair(lse_all[0], lse_all[1]), pair(lse_all[2], lse_all[3])], axis=1
    )

    def order_pair(a, b):
        return jnp.concatenate([order_all[a].astype(f32), order_all[b].astype(f32)], axis=1)

    order_lanes = jnp.concatenate([order_pair(0, 1), order_pair(2, 3)], axis=1)
    o_rows = o_all[...].reshape(RING * num_blocks, heads * head_dim)
    places = 2 * rows
    sub_p = lax.broadcasted_iota(jnp.int32, (places, lane_n), 0)
    lane_p = lax.broadcasted_iota(jnp.int32, (places, lane_n), 1)
    row8 = lax.broadcasted_iota(jnp.int32, (8, lane_n), 0)

    def column(j):
        first = (RING * places * f + places * j) * other + (RING * places * j + places * f) * core
        piece = lax.div(first, lane_n)
        offset = lax.rem(first, lane_n)
        diag = lane_p == sub_p + offset
        end = jnp.sum(jnp.where(diag, ends_ref[pl.ds(piece, 1), :], 0.0), axis=1, keepdims=True)
        start = jnp.sum(jnp.where(diag, starts_ref[pl.ds(piece, 1), :], 0.0), axis=1, keepdims=True)
        member = (start <= order_lanes) & (order_lanes < end)
        tile = jnp.zeros((8, lane_n), f32)
        for h in range(heads):
            here = jnp.where(member, lse[h:h + 1, :], VERY_LOW)
            top_r = jnp.max(here, axis=1, keepdims=True)
            w = jnp.where(member, jnp.exp(here - top_r), 0.0).astype(bf16)
            total = jnp.sum(w.astype(f32), axis=1, keepdims=True)
            acc = jnp.dot(
                w, o_rows[:, h * head_dim:(h + 1) * head_dim], preferred_element_type=f32
            )
            safe = jnp.where(total > 0.0, total, 1.0)
            tab[j, :, h * head_dim:(h + 1) * head_dim] = (acc / safe).astype(bf16)
            lse_r = jnp.where(total > 0.0, top_r + jnp.log(safe), VERY_LOW)
            row = jnp.sum(jnp.where(lane_p == sub_p, lse_r, 0.0), axis=0, keepdims=True)
            tile = jnp.where(row8 == h, row, tile)
        tab_lse[j] = tile

    def rows_of(j, c):
        return tab.at[j, pl.ds(pl.multiple_of(c * rows, rows), rows)]

    slot = core * RING + s
    arrivals = []
    j = ring(s, 2)
    column(j)
    via = [
        send(rows_of(j, core), fwd.at[0], s_up), send(tab_lse.at[j], fwd_lse.at[0], s_up),
        send(rows_of(j, other), fwd.at[1], s_dn), send(tab_lse.at[j], fwd_lse.at[1], s_dn),
    ]
    for k, same, cross in ((1, s_up, s_up_x), (-1, s_dn, s_dn_x)):
        j = ring(s, k)
        column(j)
        arrivals += [
            send(rows_of(j, core), home.at[slot], same),
            send(tab_lse.at[j], home_lse.at[slot], same),
            send(rows_of(j, other), home.at[slot], cross),
            send(tab_lse.at[j], home_lse.at[slot], cross),
        ]
    column(s)
    arrivals += [
        send(rows_of(s, other), home.at[slot], sib), send(tab_lse.at[s], home_lse.at[slot], sib)
    ]
    for copy in via:
        copy.wait_recv()
    up_slot = core * RING + ring(s, -1)
    dn_slot = core * RING + ring(s, 1)
    arrivals += [
        send(fwd.at[0], home.at[up_slot], s_up), send(fwd_lse.at[0], home_lse.at[up_slot], s_up),
        send(fwd.at[1], home.at[dn_slot], s_dn_x), send(fwd_lse.at[1], home_lse.at[dn_slot], s_dn_x),
    ]
    home[slot] = tab[s, pl.ds(pl.multiple_of(core * rows, rows), rows)]
    home_lse[slot] = tab_lse[s]
    for copy in arrivals:
        copy.wait_recv()

    sub_r = lax.broadcasted_iota(jnp.int32, (rows, lane_n), 0)
    lane_r = lax.broadcasted_iota(jnp.int32, (rows, lane_n), 1)
    diag = lane_r == sub_r + core * rows
    new_value = new_kv[:, head_dim:].astype(f32)
    attention = []
    sources = 2 * RING
    for h in range(heads):
        cols_h = [
            jnp.sum(jnp.where(diag, home_lse[n, h:h + 1, :], 0.0), axis=1, keepdims=True)
            for n in range(sources)
        ]
        top_h = own_score[h]
        for c in cols_h:
            top_h = jnp.maximum(top_h, c)
        w = jnp.exp(own_score[h] - top_h)
        mixed, denominator = w * new_value, w
        for n in range(sources):
            w = jnp.exp(cols_h[n] - top_h)
            denominator = denominator + w
            mixed = mixed + w * home[n, :, h * head_dim:(h + 1) * head_dim].astype(f32)
        attention.append((mixed / denominator).astype(bf16))
    att = jnp.concatenate(attention, axis=1)

    tp_sends = []
    for k in (2, 1, 3):
        t = lax.rem(tp + k, RING)
        part[t] = jnp.dot(att, weight[t], preferred_element_type=f32).astype(bf16)
        tp_sends.append(send(part.at[t], part_in.at[tp], tps[k - 1]))
    total = jnp.dot(att, weight[tp], preferred_element_type=f32) + residual[...].astype(f32)
    for copy in tp_sends:
        copy.wait_recv()
    for k in range(1, RING):
        total = total + part_in[lax.rem(tp + k, RING)].astype(f32)
    out_ref[...] = total.astype(bf16)

    for copy in started:
        copy.wait_send()


def local(residual, queries, new_kv, cache, out_weight, block_counts, last_fill, block_order):
    rows, cols = residual.shape
    num_blocks, block_len, width = cache.shape
    head_dim = width // 2
    q_cols = queries.shape[1]
    requests = block_counts.shape[0]
    lanes = 128
    devices = requests // rows
    any_spec = pl.BlockSpec(memory_space=pl.ANY)
    f32, bf16 = jnp.float32, jnp.bfloat16
    copies = 96
    return pl.pallas_call(
        kernel,
        out_shape=jax.ShapeDtypeStruct((rows, cols), bf16),
        in_specs=[any_spec] * 8,
        out_specs=pl.BlockSpec(memory_space=pltpu.VMEM),
        scratch_shapes=[
            pltpu.VMEM(cache.shape, bf16),
            pltpu.VMEM((RING, q_cols, cols), bf16),
            pltpu.VMEM((rows, cols), bf16),
            pltpu.VMEM((rows, width), bf16),
            pltpu.VMEM((rows, q_cols), bf16),
            pltpu.VMEM((requests // lanes, lanes), jnp.int32),
            pltpu.VMEM((requests // lanes, lanes), jnp.int32),
            pltpu.VMEM((RING, 1, num_blocks), jnp.int32),
            pltpu.VMEM((devices, rows, q_cols), bf16),
            pltpu.VMEM((requests // lanes, lanes), f32),
            pltpu.VMEM((requests // lanes, lanes), f32),
            pltpu.VMEM((num_blocks, requests), bf16),
            pltpu.VMEM((num_blocks, 8, head_dim), f32),
            pltpu.VMEM((num_blocks, 8, block_len), f32),
            pltpu.VMEM((num_blocks, 8, head_dim), f32),
            pltpu.VMEM((RING, GROUPS, num_blocks // GROUPS, q_cols), bf16),
            pltpu.VMEM((RING, 8, lanes), f32),
            pltpu.VMEM((RING, 2 * rows, q_cols), bf16),
            pltpu.VMEM((RING, 8, lanes), f32),
            pltpu.VMEM((2, rows, q_cols), bf16),
            pltpu.VMEM((2, 8, lanes), f32),
            pltpu.VMEM((2 * RING, rows, q_cols), bf16),
            pltpu.VMEM((2 * RING, 8, lanes), f32),
            pltpu.VMEM((RING, rows, cols), bf16),
            pltpu.VMEM((RING, rows, cols), bf16),
            pltpu.SemaphoreType.DMA((copies,)),
            pltpu.SemaphoreType.DMA((copies,)),
            pltpu.SemaphoreType.DMA((8,)),
            pltpu.SemaphoreType.DMA((11,)),
        ],
        compiler_params=pltpu.CompilerParams(
            collective_id=0, has_side_effects=True, vmem_limit_bytes=60 * 1024 * 1024
        ),
    )(
        block_order.reshape(1, num_blocks),
        block_counts.reshape(requests // lanes, lanes),
        last_fill.reshape(requests // lanes, lanes),
        residual, queries, new_kv, cache, out_weight,
    )


def solution(mesh):
    in_specs = (
        P("seq", "tp"), P("seq", "tp"), P("seq", None), P("seq", None, None), P("tp", None),
        P(), P(), P("seq"),
    )
    return jax.shard_map(
        local, mesh=mesh, in_specs=in_specs, out_specs=P("seq", "tp"), check_vma=False
    )
```

```python
import jax
import jax.numpy as jnp
from jax import lax
from jax.experimental import pallas as pl
from jax.experimental.pallas import tpu as pltpu
from jax.sharding import PartitionSpec as P

MESH = pl.DeviceIdType.MESH
VERY_LOW = -1e30
RING = 4
GROUPS = 4


def kernel(
    order_hbm, counts_hbm, fill_hbm, residual_hbm, queries_hbm, new_kv_hbm, cache_hbm, weight_hbm,
    out_ref,
    cache, weight, residual, new_kv, q_own, counts, fill, order_all, q_all, ends_ref, starts_ref,
    onehot_ref, order_sib, pick_out, pick_in, q_blk, live, o_scr, o_all, lse_all, tab, tab_lse,
    home, home_lse, part, part_in, send_sem, recv_sem, cache_sem, local_sem,
):
    num_blocks, block_len, width = cache.shape
    head_dim = width // 2
    rows = q_own.shape[0]
    heads = q_own.shape[1] // head_dim
    cols = residual.shape[1]
    per_group = num_blocks // GROUPS
    inv_root = 1.0 / head_dim**0.5
    f32, bf16 = jnp.float32, jnp.bfloat16

    me = lax.axis_index("seq")
    tp = lax.axis_index("tp")
    core = lax.rem(me, 2)
    other = 1 - core
    chip = lax.div(me, 2)
    x = lax.div(chip, RING)
    z = lax.rem(chip, RING)
    f = x * other + z * core
    s = z * other + x * core

    def seq_of(fi, si, ci):
        xi = fi * other + si * core
        zi = si * other + fi * core
        return (xi * RING + zi) * 2 + ci

    def ring(a, k):
        return lax.rem(a + k + RING, RING)

    f_up = (seq_of(ring(f, 1), s, core), tp)
    f_dn = (seq_of(ring(f, -1), s, core), tp)
    s_up = (seq_of(f, ring(s, 1), core), tp)
    s_dn = (seq_of(f, ring(s, -1), core), tp)
    s_up_x = (seq_of(f, ring(s, 1), other), tp)
    s_dn_x = (seq_of(f, ring(s, -1), other), tp)
    f_2 = (seq_of(ring(f, 2), s, core), tp)
    s_2 = (seq_of(f, ring(s, 2), core), tp)
    s_2_x = (seq_of(f, ring(s, 2), other), tp)
    f_up_x = (seq_of(ring(f, 1), s, other), tp)
    f_dn_x = (seq_of(ring(f, -1), s, other), tp)
    f_2_x = (seq_of(ring(f, 2), s, other), tp)
    sib = (seq_of(f, s, other), tp)
    tps = [(me, lax.rem(tp + k, RING)) for k in range(1, RING)]

    barrier = pltpu.get_barrier_semaphore()
    peers = [
        f_up, f_dn, f_2, s_up, s_dn, s_2, f_up_x, f_dn_x, f_2_x, s_up_x, s_dn_x, s_2_x, sib
    ] + tps
    for peer in peers:
        pl.semaphore_signal(barrier, inc=1, device_id=peer, device_id_type=MESH)

    own_q = pltpu.make_async_copy(queries_hbm, q_own, local_sem.at[0])
    own_q.start()
    small = [
        pltpu.make_async_copy(order_hbm, order_all.at[f], local_sem.at[1]),
        pltpu.make_async_copy(counts_hbm, counts, local_sem.at[2]),
        pltpu.make_async_copy(fill_hbm, fill, local_sem.at[3]),
        pltpu.make_async_copy(new_kv_hbm, new_kv, local_sem.at[4]),
        pltpu.make_async_copy(residual_hbm, residual, local_sem.at[5]),
        pltpu.make_async_copy(queries_hbm, q_all.at[me], local_sem.at[6]),
    ]
    for copy in small:
        copy.start()

    cache_copies = [
        pltpu.make_async_copy(
            cache_hbm.at[pl.ds(i * per_group, per_group)],
            cache.at[pl.ds(i * per_group, per_group)],
            cache_sem.at[i],
        )
        for i in range(GROUPS)
    ]
    for copy in cache_copies:
        copy.start()
    weight_copies = [
        pltpu.make_async_copy(
            weight_hbm.at[:, pl.ds(t * cols, cols)], weight.at[t], local_sem.at[7]
        )
        for t in range(RING)
    ]
    for copy in weight_copies:
        copy.start()

    def send(src, dst, peer, ss, rs):
        copy = pltpu.make_async_remote_copy(
            src_ref=src, dst_ref=dst, send_sem=send_sem.at[ss], recv_sem=recv_sem.at[rs],
            device_id=peer, device_id_type=MESH,
        )
        copy.start()
        return copy

    def wait_bytes(ref, sem):
        pltpu.make_async_copy(ref, ref, sem).wait()

    own_q.wait()
    pl.semaphore_wait(barrier, len(peers))

    half = rows // 2
    top, bottom = pl.ds(0, half), pl.ds(half, half)

    def chunk(i, j):
        return q_all.at[seq_of(ring(f, i), ring(s, j), core)]

    def part_of(i, j, which):
        return q_all.at[seq_of(ring(f, i), ring(s, j), core), which]

    def to_s(i, src=None):
        c = chunk(i, 0)
        src = c if src is None else src
        n = 3 + 2 * (i % RING)
        return (send(src, c, s_up, 0, n), send(src, c, s_dn, 0, n + 1))

    own_up = send(q_own, chunk(0, 0), f_up, 0, 0)
    own_dn = send(q_own, chunk(0, 0), f_dn, 0, 1)
    own_2 = send(q_own, chunk(0, 0), f_2, 0, 2)
    s_copies = {0: to_s(0, q_own)}

    for copy in small:
        copy.wait()
    order_own = order_all.at[f]
    order_to_sib = send(order_own, order_sib, sib, 1, 12)
    order_copies = [
        send(order_own, order_own, peer, 2 + k, 13 + k) for k, peer in enumerate((f_up, f_dn, f_2))
    ]

    counts_f = counts[...].astype(f32)
    fill_f = fill[...].astype(f32)
    lane_n = counts_f.shape[1]
    sub_i = lax.broadcasted_iota(jnp.int32, (lane_n, lane_n), 0)
    lane_i = lax.broadcasted_iota(jnp.int32, (lane_n, lane_n), 1)
    upper = (sub_i <= lane_i).astype(f32).astype(bf16)
    cum = jnp.dot(counts_f.astype(bf16), upper, preferred_element_type=f32)
    before = jnp.zeros((1, 1), f32)
    pieces = counts_f.shape[0]
    for k in range(pieces):
        ends_k = cum[k:k + 1, :] + before
        ends_ref[k:k + 1, :] = ends_k
        starts_ref[k:k + 1, :] = ends_k - counts_f[k:k + 1, :]
        before = before + jnp.sum(counts_f[k:k + 1, :], axis=1, keepdims=True)

    sub64 = lax.broadcasted_iota(jnp.int32, (num_blocks, num_blocks), 0)
    lane64 = lax.broadcasted_iota(jnp.int32, (num_blocks, num_blocks), 1)

    def column_of(order_row):
        return jnp.sum(
            jnp.where(
                sub64 == lane64, jnp.broadcast_to(order_row, (num_blocks, num_blocks)), 0.0
            ),
            axis=1, keepdims=True,
        )

    order_col = column_of(order_all[f].astype(f32))
    fill_raw = jnp.zeros((num_blocks, lane_n), f32)
    for k in range(pieces):
        ends_k = ends_ref[k:k + 1, :]
        starts_k = starts_ref[k:k + 1, :]
        hit = (starts_k <= order_col) & (order_col < ends_k)
        onehot_ref[0, :, k * lane_n:(k + 1) * lane_n] = jnp.where(hit, 1.0, 0.0).astype(bf16)
        fill_raw = fill_raw + jnp.where(ends_k == order_col + 1.0, fill_f[k:k + 1, :], 0.0)
    fill_sum = jnp.sum(fill_raw, axis=1, keepdims=True)
    live_n = jnp.where(fill_sum > 0.0, fill_sum, float(block_len))
    order_to_sib.wait_recv()
    order_col = column_of(order_sib[...].astype(f32))
    for k in range(pieces):
        hit = (starts_ref[k:k + 1, :] <= order_col) & (order_col < ends_ref[k:k + 1, :])
        onehot_ref[1, :, k * lane_n:(k + 1) * lane_n] = jnp.where(hit, 1.0, 0.0).astype(bf16)
    for n in range(RING * RING):
        q_all[2 * n + other] = jnp.zeros((rows, heads * head_dim), bf16)
    for h in range(8):
        live[:, h, :] = jnp.broadcast_to(live_n, (num_blocks, block_len))
    q_blk[...] = jnp.zeros(q_blk.shape, f32)

    def forward_s(i):
        up, dn = s_copies[i]
        up.wait_recv()
        send(part_of(i, -1, top), part_of(i, -1, top), s_up, 0, 11)
        dn.wait_recv()
        send(part_of(i, 1, bottom), part_of(i, 1, bottom), s_dn, 0, 11)

    own_up.wait_recv()
    s_copies[-1] = to_s(-1)
    own_dn.wait_recv()
    s_copies[1] = to_s(1)
    forward_s(0)
    own_2.wait_recv()
    s_copies[2] = to_s(2)
    forward_s(-1)
    forward_s(1)
    forward_s(2)
    wait_bytes(q_all.at[pl.ds(0, RING)], recv_sem.at[11])

    q_rows = q_all[...].reshape(q_all.shape[0] * rows, heads * head_dim)
    pick_out[...] = jnp.dot(onehot_ref[1], q_rows, preferred_element_type=f32).astype(bf16)
    pick = send(pick_out, pick_in, sib, 5, 16)
    picked = jnp.dot(onehot_ref[0], q_rows, preferred_element_type=f32)
    pick.wait_recv()
    picked = picked + pick_in[...].astype(f32)
    for h in range(heads):
        q_blk[:, h, :] = picked[:, h * head_dim:(h + 1) * head_dim]

    lse_all[f] = jnp.zeros((8, lane_n), f32)
    token = lax.broadcasted_iota(jnp.int32, (8, block_len), 1).astype(f32)
    lane8 = lax.broadcasted_iota(jnp.int32, (8, lane_n), 1)

    for g in range(GROUPS):
        cache_copies[g].wait()
        blocks = range(g * per_group, (g + 1) * per_group)
        lse_rows = lse_all[f]
        scores = []
        for b in blocks:
            q8 = q_blk[b].astype(bf16)
            scores.append(
                lax.dot_general(
                    q8, cache[b, :, :head_dim], (((1,), (1,)), ((), ())), preferred_element_type=f32
                )
            )
        for b, score in zip(blocks, scores):
            alive = token < live[b]
            score = jnp.where(alive, score * inv_root, VERY_LOW)
            top_b = jnp.max(score, axis=1, keepdims=True)
            w = jnp.where(alive, jnp.exp(score - top_b), 0.0)
            total = jnp.sum(w, axis=1, keepdims=True)
            acc = jnp.dot(w.astype(bf16), cache[b, :, head_dim:], preferred_element_type=f32)
            o_scr[b] = acc / total
            lse_rows = jnp.where(lane8 == b, top_b + jnp.log(total), lse_rows)
        lse_all[f] = lse_rows
        for h in range(heads):
            o_all[f, g, :, h * head_dim:(h + 1) * head_dim] = (
                o_scr[g * per_group:(g + 1) * per_group, h, :].astype(bf16)
            )
        ref = o_all.at[f, g]
        for peer in (f_2, f_up, f_dn):
            send(ref, ref, peer, 6, 17)
    ref = lse_all.at[f]
    for peer in (f_2, f_up, f_dn):
        send(ref, ref, peer, 7, 18)

    q_f = q_own[...].astype(f32)
    new_key = new_kv[:, :head_dim].astype(f32)
    own_score = [
        jnp.sum(q_f[:, h * head_dim:(h + 1) * head_dim] * new_key, axis=1, keepdims=True) * inv_root
        for h in range(heads)
    ]
    wait_bytes(weight, local_sem.at[7])
    for copy in order_copies:
        copy.wait_recv()
    wait_bytes(lse_all.at[pl.ds(0, RING - 1)], recv_sem.at[18])
    wait_bytes(o_all.at[pl.ds(0, RING - 1)], recv_sem.at[17])

    def pair(a, b):
        lanes = lax.broadcasted_iota(jnp.int32, a.shape, 1)
        return jnp.where(lanes < num_blocks, a, pltpu.roll(b, num_blocks, 1))

    lse = jnp.concatenate(
        [pair(lse_all[0], lse_all[1]), pair(lse_all[2], lse_all[3])], axis=1
    )

    def order_pair(a, b):
        return jnp.concatenate([order_all[a].astype(f32), order_all[b].astype(f32)], axis=1)

    order_lanes = jnp.concatenate([order_pair(0, 1), order_pair(2, 3)], axis=1)
    o_rows = o_all[...].reshape(RING * num_blocks, heads * head_dim)
    places = 2 * rows
    sub_p = lax.broadcasted_iota(jnp.int32, (places, lane_n), 0)
    lane_p = lax.broadcasted_iota(jnp.int32, (places, lane_n), 1)
    row8 = lax.broadcasted_iota(jnp.int32, (8, lane_n), 0)

    def column(j):
        first = (RING * places * f + places * j) * other + (RING * places * j + places * f) * core
        piece = lax.div(first, lane_n)
        offset = lax.rem(first, lane_n)
        diag = lane_p == sub_p + offset
        end = jnp.sum(jnp.where(diag, ends_ref[pl.ds(piece, 1), :], 0.0), axis=1, keepdims=True)
        start = jnp.sum(jnp.where(diag, starts_ref[pl.ds(piece, 1), :], 0.0), axis=1, keepdims=True)
        member = (start <= order_lanes) & (order_lanes < end)
        tile = jnp.zeros((8, lane_n), f32)
        for h in range(heads):
            here = jnp.where(member, lse[h:h + 1, :], VERY_LOW)
            top_r = jnp.max(here, axis=1, keepdims=True)
            w = jnp.where(member, jnp.exp(here - top_r), 0.0).astype(bf16)
            total = jnp.sum(w.astype(f32), axis=1, keepdims=True)
            acc = jnp.dot(
                w, o_rows[:, h * head_dim:(h + 1) * head_dim], preferred_element_type=f32
            )
            safe = jnp.where(total > 0.0, total, 1.0)
            tab[j, :, h * head_dim:(h + 1) * head_dim] = (acc / safe).astype(bf16)
            lse_r = jnp.where(total > 0.0, top_r + jnp.log(safe), VERY_LOW)
            row = jnp.sum(jnp.where(lane_p == sub_p, lse_r, 0.0), axis=0, keepdims=True)
            tile = jnp.where(row8 == h, row, tile)
        tab_lse[j] = tile

    def rows_of(j, c):
        return tab.at[j, pl.ds(pl.multiple_of(c * rows, rows), rows)]

    slot = core * RING + s
    for k, same, cross in ((2, s_2, s_2_x), (1, s_up, s_up_x), (-1, s_dn, s_dn_x)):
        j = ring(s, k)
        column(j)
        send(rows_of(j, core), home.at[slot], same, 8, 19)
        send(tab_lse.at[j], home_lse.at[slot], same, 9, 20)
        send(rows_of(j, other), home.at[slot], cross, 8, 19)
        send(tab_lse.at[j], home_lse.at[slot], cross, 9, 20)
    column(s)
    send(rows_of(s, other), home.at[slot], sib, 8, 19)
    send(tab_lse.at[s], home_lse.at[slot], sib, 9, 20)
    home[slot] = tab[s, pl.ds(pl.multiple_of(core * rows, rows), rows)]
    home_lse[slot] = tab_lse[s]
    sources = 2 * RING
    wait_bytes(home_lse.at[pl.ds(0, sources - 1)], recv_sem.at[20])
    wait_bytes(home.at[pl.ds(0, sources - 1)], recv_sem.at[19])

    sub_r = lax.broadcasted_iota(jnp.int32, (rows, lane_n), 0)
    lane_r = lax.broadcasted_iota(jnp.int32, (rows, lane_n), 1)
    diag = lane_r == sub_r + core * rows
    new_value = new_kv[:, head_dim:].astype(f32)
    attention = []
    for h in range(heads):
        cols_h = [
            jnp.sum(jnp.where(diag, home_lse[n, h:h + 1, :], 0.0), axis=1, keepdims=True)
            for n in range(sources)
        ]
        top_h = own_score[h]
        for c in cols_h:
            top_h = jnp.maximum(top_h, c)
        w = jnp.exp(own_score[h] - top_h)
        mixed, denominator = w * new_value, w
        for n in range(sources):
            w = jnp.exp(cols_h[n] - top_h)
            denominator = denominator + w
            mixed = mixed + w * home[n, :, h * head_dim:(h + 1) * head_dim].astype(f32)
        attention.append((mixed / denominator).astype(bf16))
    att = jnp.concatenate(attention, axis=1)

    for k in (2, 1, 3):
        t = lax.rem(tp + k, RING)
        part[t] = jnp.dot(att, weight[t], preferred_element_type=f32).astype(bf16)
        send(part.at[t], part_in.at[tp], tps[k - 1], 10, 21)
    total = jnp.dot(att, weight[tp], preferred_element_type=f32) + residual[...].astype(f32)
    wait_bytes(part_in.at[pl.ds(0, RING - 1)], recv_sem.at[21])
    for k in range(1, RING):
        total = total + part_in[lax.rem(tp + k, RING)].astype(f32)
    out_ref[...] = total.astype(bf16)

    wait_bytes(q_all.at[pl.ds(0, 15)], send_sem.at[0])
    order_to_sib.wait_send()
    for copy in order_copies:
        copy.wait_send()
    pick.wait_send()
    wait_bytes(o_all.at[pl.ds(0, RING - 1)], send_sem.at[6])
    wait_bytes(lse_all.at[pl.ds(0, RING - 1)], send_sem.at[7])
    wait_bytes(home.at[pl.ds(0, sources - 1)], send_sem.at[8])
    wait_bytes(home_lse.at[pl.ds(0, sources - 1)], send_sem.at[9])
    wait_bytes(part_in.at[pl.ds(0, RING - 1)], send_sem.at[10])


def local(residual, queries, new_kv, cache, out_weight, block_counts, last_fill, block_order):
    rows, cols = residual.shape
    num_blocks, block_len, width = cache.shape
    head_dim = width // 2
    q_cols = queries.shape[1]
    requests = block_counts.shape[0]
    lanes = 128
    devices = requests // rows
    any_spec = pl.BlockSpec(memory_space=pl.ANY)
    f32, bf16 = jnp.float32, jnp.bfloat16
    return pl.pallas_call(
        kernel,
        out_shape=jax.ShapeDtypeStruct((rows, cols), bf16),
        in_specs=[any_spec] * 8,
        out_specs=pl.BlockSpec(memory_space=pltpu.VMEM),
        scratch_shapes=[
            pltpu.VMEM(cache.shape, bf16),
            pltpu.VMEM((RING, q_cols, cols), bf16),
            pltpu.VMEM((rows, cols), bf16),
            pltpu.VMEM((rows, width), bf16),
            pltpu.VMEM((rows, q_cols), bf16),
            pltpu.VMEM((requests // lanes, lanes), jnp.int32),
            pltpu.VMEM((requests // lanes, lanes), jnp.int32),
            pltpu.VMEM((RING, 1, num_blocks), jnp.int32),
            pltpu.VMEM((devices, rows, q_cols), bf16),
            pltpu.VMEM((requests // lanes, lanes), f32),
            pltpu.VMEM((requests // lanes, lanes), f32),
            pltpu.VMEM((2, num_blocks, requests), bf16),
            pltpu.VMEM((1, num_blocks), jnp.int32),
            pltpu.VMEM((num_blocks, q_cols), bf16),
            pltpu.VMEM((num_blocks, q_cols), bf16),
            pltpu.VMEM((num_blocks, 8, head_dim), f32),
            pltpu.VMEM((num_blocks, 8, block_len), f32),
            pltpu.VMEM((num_blocks, 8, head_dim), f32),
            pltpu.VMEM((RING, GROUPS, num_blocks // GROUPS, q_cols), bf16),
            pltpu.VMEM((RING, 8, lanes), f32),
            pltpu.VMEM((RING, 2 * rows, q_cols), bf16),
            pltpu.VMEM((RING, 8, lanes), f32),
            pltpu.VMEM((2 * RING, rows, q_cols), bf16),
            pltpu.VMEM((2 * RING, 8, lanes), f32),
            pltpu.VMEM((RING, rows, cols), bf16),
            pltpu.VMEM((RING, rows, cols), bf16),
            pltpu.SemaphoreType.DMA((11,)),
            pltpu.SemaphoreType.DMA((22,)),
            pltpu.SemaphoreType.DMA((GROUPS,)),
            pltpu.SemaphoreType.DMA((8,)),
        ],
        compiler_params=pltpu.CompilerParams(
            collective_id=0, has_side_effects=True, vmem_limit_bytes=60 * 1024 * 1024
        ),
    )(
        block_order.reshape(1, num_blocks),
        block_counts.reshape(requests // lanes, lanes),
        last_fill.reshape(requests // lanes, lanes),
        residual, queries, new_kv, cache, out_weight,
    )


def solution(mesh):
    in_specs = (
        P("seq", "tp"), P("seq", "tp"), P("seq", None), P("seq", None, None), P("tp", None),
        P(), P(), P("seq"),
    )
    return jax.shard_map(
        local, mesh=mesh, in_specs=in_specs, out_specs=P("seq", "tp"), check_vma=False
    )
```

```python
import jax
import jax.numpy as jnp
from jax import lax
from jax.experimental import pallas as pl
from jax.experimental.pallas import tpu as pltpu
from jax.sharding import PartitionSpec as P

MESH = pl.DeviceIdType.MESH
VERY_LOW = -1e30
RING = 4
GROUPS = 4


def kernel(
    order_hbm, counts_hbm, fill_hbm, residual_hbm, queries_hbm, new_kv_hbm, cache_hbm, weight_hbm,
    out_ref,
    cache, weight, residual, new_kv, q_own, counts, fill, order_all, q_rel, ends_ref, starts_ref,
    onehot_ref, early_ref, order_sib, pick_out, pick_in, q_blk, live, o_scr, o_all, lse_all, tab, tab_lse,
    home, home_lse, part, part_in, send_sem, recv_sem, cache_sem, local_sem,
):
    num_blocks, block_len, width = cache.shape
    head_dim = width // 2
    rows = q_own.shape[0]
    heads = q_own.shape[1] // head_dim
    cols = residual.shape[1]
    per_group = num_blocks // GROUPS
    inv_root = 1.0 / head_dim**0.5
    f32, bf16 = jnp.float32, jnp.bfloat16

    me = lax.axis_index("seq")
    tp = lax.axis_index("tp")
    core = lax.rem(me, 2)
    other = 1 - core
    chip = lax.div(me, 2)
    x = lax.div(chip, RING)
    z = lax.rem(chip, RING)
    f = x * other + z * core
    s = z * other + x * core

    def seq_of(fi, si, ci):
        xi = fi * other + si * core
        zi = si * other + fi * core
        return (xi * RING + zi) * 2 + ci

    def ring(a, k):
        return lax.rem(a + k + RING, RING)

    f_up = (seq_of(ring(f, 1), s, core), tp)
    f_dn = (seq_of(ring(f, -1), s, core), tp)
    s_up = (seq_of(f, ring(s, 1), core), tp)
    s_dn = (seq_of(f, ring(s, -1), core), tp)
    s_up_x = (seq_of(f, ring(s, 1), other), tp)
    s_dn_x = (seq_of(f, ring(s, -1), other), tp)
    f_2 = (seq_of(ring(f, 2), s, core), tp)
    s_2 = (seq_of(f, ring(s, 2), core), tp)
    s_2_x = (seq_of(f, ring(s, 2), other), tp)
    f_up_x = (seq_of(ring(f, 1), s, other), tp)
    f_dn_x = (seq_of(ring(f, -1), s, other), tp)
    f_2_x = (seq_of(ring(f, 2), s, other), tp)
    sib = (seq_of(f, s, other), tp)
    tps = [(me, lax.rem(tp + k, RING)) for k in range(1, RING)]

    barrier = pltpu.get_barrier_semaphore()
    peers = [
        f_up, f_dn, f_2, s_up, s_dn, s_2, f_up_x, f_dn_x, f_2_x, s_up_x, s_dn_x, s_2_x, sib
    ] + tps
    for peer in peers:
        pl.semaphore_signal(barrier, inc=1, device_id=peer, device_id_type=MESH)

    own_q = pltpu.make_async_copy(queries_hbm, q_own, local_sem.at[0])
    own_q.start()
    small = [
        pltpu.make_async_copy(order_hbm, order_all.at[f], local_sem.at[1]),
        pltpu.make_async_copy(counts_hbm, counts, local_sem.at[2]),
        pltpu.make_async_copy(fill_hbm, fill, local_sem.at[3]),
        pltpu.make_async_copy(new_kv_hbm, new_kv, local_sem.at[4]),
        pltpu.make_async_copy(residual_hbm, residual, local_sem.at[5]),
        pltpu.make_async_copy(queries_hbm, q_rel.at[0], local_sem.at[6]),
    ]
    for copy in small:
        copy.start()

    cache_copies = [
        pltpu.make_async_copy(
            cache_hbm.at[pl.ds(i * per_group, per_group)],
            cache.at[pl.ds(i * per_group, per_group)],
            cache_sem.at[i],
        )
        for i in range(GROUPS)
    ]
    for copy in cache_copies:
        copy.start()
    weight_copies = [
        pltpu.make_async_copy(
            weight_hbm.at[:, pl.ds(t * cols, cols)], weight.at[t], local_sem.at[7]
        )
        for t in range(RING)
    ]
    for copy in weight_copies:
        copy.start()

    def send(src, dst, peer, ss, rs):
        copy = pltpu.make_async_remote_copy(
            src_ref=src, dst_ref=dst, send_sem=send_sem.at[ss], recv_sem=recv_sem.at[rs],
            device_id=peer, device_id_type=MESH,
        )
        copy.start()
        return copy

    def wait_bytes(ref, sem):
        pltpu.make_async_copy(ref, ref, sem).wait()

    own_q.wait()
    pl.semaphore_wait(barrier, len(peers))

    half = rows // 2
    top, bottom = pl.ds(0, half), pl.ds(half, half)

    def place(i, j):
        return (0, 2, 3, 1)[j % RING] * RING + i % RING

    def to_s(i, src=None):
        src = q_rel.at[place(i, 0)] if src is None else src
        n = 3 + 2 * (i % RING)
        return (
            send(src, q_rel.at[place(i, -1)], s_up, 0, n),
            send(src, q_rel.at[place(i, 1)], s_dn, 0, n + 1),
        )

    own_up = send(q_own, q_rel.at[place(-1, 0)], f_up, 0, 0)
    own_dn = send(q_own, q_rel.at[place(1, 0)], f_dn, 0, 1)
    own_2 = send(q_own, q_rel.at[place(2, 0)], f_2, 0, 2)
    s_copies = {0: to_s(0, q_own)}

    for copy in small:
        copy.wait()
    order_own = order_all.at[f]
    order_to_sib = send(order_own, order_sib, sib, 1, 12)
    order_copies = [
        send(order_own, order_own, peer, 2 + k, 13 + k) for k, peer in enumerate((f_up, f_dn, f_2))
    ]

    counts_f = counts[...].astype(f32)
    fill_f = fill[...].astype(f32)
    lane_n = counts_f.shape[1]
    sub_i = lax.broadcasted_iota(jnp.int32, (lane_n, lane_n), 0)
    lane_i = lax.broadcasted_iota(jnp.int32, (lane_n, lane_n), 1)
    upper = (sub_i <= lane_i).astype(f32).astype(bf16)
    cum = jnp.dot(counts_f.astype(bf16), upper, preferred_element_type=f32)
    before = jnp.zeros((1, 1), f32)
    pieces = counts_f.shape[0]
    for k in range(pieces):
        ends_k = cum[k:k + 1, :] + before
        ends_ref[k:k + 1, :] = ends_k
        starts_ref[k:k + 1, :] = ends_k - counts_f[k:k + 1, :]
        before = before + jnp.sum(counts_f[k:k + 1, :], axis=1, keepdims=True)

    sub64 = lax.broadcasted_iota(jnp.int32, (num_blocks, num_blocks), 0)
    lane64 = lax.broadcasted_iota(jnp.int32, (num_blocks, num_blocks), 1)

    def column_of(order_row):
        return jnp.sum(
            jnp.where(
                sub64 == lane64, jnp.broadcast_to(order_row, (num_blocks, num_blocks)), 0.0
            ),
            axis=1, keepdims=True,
        )

    row_lane = lax.broadcasted_iota(jnp.int32, (num_blocks, RING * rows), 1)
    row_ids = []
    for j in (0, -1, 1, 2):
        ids = row_lane
        for i in range(RING):
            base = seq_of(ring(f, i), ring(s, j), core) * rows - i * rows
            here = (row_lane >= i * rows) & (row_lane < (i + 1) * rows)
            ids = jnp.where(here, row_lane + base, ids)
        row_ids.append(ids.astype(f32))

    def select(which, order_col):
        passed = jnp.zeros((num_blocks, lane_n), f32)
        for k in range(pieces):
            passed = passed + jnp.where(ends_ref[k:k + 1, :] <= order_col, 1.0, 0.0)
        request = jnp.sum(passed, axis=1, keepdims=True)
        for n in range(RING):
            onehot_ref[which, :, n * RING * rows:(n + 1) * RING * rows] = (
                jnp.where(row_ids[n] == request, 1.0, 0.0).astype(bf16)
            )

    order_col = column_of(order_all[f].astype(f32))
    fill_raw = jnp.zeros((num_blocks, lane_n), f32)
    for k in range(pieces):
        fill_raw = fill_raw + jnp.where(
            ends_ref[k:k + 1, :] == order_col + 1.0, fill_f[k:k + 1, :], 0.0
        )
    fill_sum = jnp.sum(fill_raw, axis=1, keepdims=True)
    live_n = jnp.where(fill_sum > 0.0, fill_sum, float(block_len))
    select(0, order_col)
    order_to_sib.wait_recv()
    select(1, column_of(order_sib[...].astype(f32)))
    for h in range(8):
        live[:, h, :] = jnp.broadcast_to(live_n, (num_blocks, block_len))
    q_blk[...] = jnp.zeros(q_blk.shape, f32)

    def forward_s(i):
        up, dn = s_copies[i]
        up.wait_recv()
        send(q_rel.at[place(i, -1), top], q_rel.at[place(i, 2), top], s_up, 0, 11)
        dn.wait_recv()
        send(q_rel.at[place(i, 1), bottom], q_rel.at[place(i, 2), bottom], s_dn, 0, 11)

    own_up.wait_recv()
    s_copies[-1] = to_s(-1)
    own_dn.wait_recv()
    s_copies[1] = to_s(1)
    forward_s(0)
    own_2.wait_recv()
    s_copies[2] = to_s(2)
    forward_s(-1)
    forward_s(1)
    forward_s(2)

    early_n = (RING - 1) * RING
    early = q_rel[0:early_n].reshape(early_n * rows, heads * head_dim)
    for which in range(2):
        early_ref[which] = jnp.dot(
            onehot_ref[which, :, :early_n * rows], early, preferred_element_type=f32
        )
    wait_bytes(q_rel.at[pl.ds(0, RING)], recv_sem.at[11])
    late = q_rel[early_n:].reshape(RING * rows, heads * head_dim)

    def pick(which):
        return early_ref[which] + jnp.dot(
            onehot_ref[which, :, early_n * rows:], late, preferred_element_type=f32
        )

    pick_out[...] = pick(1).astype(bf16).reshape(pick_out.shape)
    picks = [send(pick_out.at[g], pick_in.at[g], sib, 5, 16 + g) for g in range(GROUPS)]
    early_ref[0] = pick(0)

    lse_all[f] = jnp.zeros((8, lane_n), f32)
    token = lax.broadcasted_iota(jnp.int32, (8, block_len), 1).astype(f32)
    lane8 = lax.broadcasted_iota(jnp.int32, (8, lane_n), 1)

    for g in range(GROUPS):
        cache_copies[g].wait()
        picks[g].wait_recv()
        first = g * per_group
        picked = early_ref[0, first:first + per_group, :] + pick_in[g].astype(f32)
        for h in range(heads):
            q_blk[first:first + per_group, h, :] = picked[:, h * head_dim:(h + 1) * head_dim]
        blocks = range(g * per_group, (g + 1) * per_group)
        lse_rows = lse_all[f]
        scores = []
        for b in blocks:
            q8 = q_blk[b].astype(bf16)
            scores.append(
                lax.dot_general(
                    q8, cache[b, :, :head_dim], (((1,), (1,)), ((), ())), preferred_element_type=f32
                )
            )
        for b, score in zip(blocks, scores):
            alive = token < live[b]
            score = jnp.where(alive, score * inv_root, VERY_LOW)
            top_b = jnp.max(score, axis=1, keepdims=True)
            w = jnp.where(alive, jnp.exp(score - top_b), 0.0)
            total = jnp.sum(w, axis=1, keepdims=True)
            acc = jnp.dot(w.astype(bf16), cache[b, :, head_dim:], preferred_element_type=f32)
            o_scr[b] = acc / total
            lse_rows = jnp.where(lane8 == b, top_b + jnp.log(total), lse_rows)
        lse_all[f] = lse_rows
        for h in range(heads):
            o_all[f, g, :, h * head_dim:(h + 1) * head_dim] = (
                o_scr[g * per_group:(g + 1) * per_group, h, :].astype(bf16)
            )
        ref = o_all.at[f, g]
        for peer in (f_2, f_up, f_dn):
            send(ref, ref, peer, 6, 20)
    ref = lse_all.at[f]
    for peer in (f_2, f_up, f_dn):
        send(ref, ref, peer, 7, 21)

    q_f = q_own[...].astype(f32)
    new_key = new_kv[:, :head_dim].astype(f32)
    own_score = [
        jnp.sum(q_f[:, h * head_dim:(h + 1) * head_dim] * new_key, axis=1, keepdims=True) * inv_root
        for h in range(heads)
    ]
    wait_bytes(weight, local_sem.at[7])
    for copy in order_copies:
        copy.wait_recv()
    wait_bytes(lse_all.at[pl.ds(0, RING - 1)], recv_sem.at[21])
    wait_bytes(o_all.at[pl.ds(0, RING - 1)], recv_sem.at[20])

    def pair(a, b):
        lanes = lax.broadcasted_iota(jnp.int32, a.shape, 1)
        return jnp.where(lanes < num_blocks, a, pltpu.roll(b, num_blocks, 1))

    lse = jnp.concatenate(
        [pair(lse_all[0], lse_all[1]), pair(lse_all[2], lse_all[3])], axis=1
    )

    def order_pair(a, b):
        return jnp.concatenate([order_all[a].astype(f32), order_all[b].astype(f32)], axis=1)

    order_lanes = jnp.concatenate([order_pair(0, 1), order_pair(2, 3)], axis=1)
    o_rows = o_all[...].reshape(RING * num_blocks, heads * head_dim)
    places = 2 * rows
    sub_p = lax.broadcasted_iota(jnp.int32, (places, lane_n), 0)
    lane_p = lax.broadcasted_iota(jnp.int32, (places, lane_n), 1)
    row8 = lax.broadcasted_iota(jnp.int32, (8, lane_n), 0)

    def column(j):
        first = (RING * places * f + places * j) * other + (RING * places * j + places * f) * core
        piece = lax.div(first, lane_n)
        offset = lax.rem(first, lane_n)
        diag = lane_p == sub_p + offset
        end = jnp.sum(jnp.where(diag, ends_ref[pl.ds(piece, 1), :], 0.0), axis=1, keepdims=True)
        start = jnp.sum(jnp.where(diag, starts_ref[pl.ds(piece, 1), :], 0.0), axis=1, keepdims=True)
        member = (start <= order_lanes) & (order_lanes < end)
        tile = jnp.zeros((8, lane_n), f32)
        for h in range(heads):
            here = jnp.where(member, lse[h:h + 1, :], VERY_LOW)
            top_r = jnp.max(here, axis=1, keepdims=True)
            w = jnp.where(member, jnp.exp(here - top_r), 0.0).astype(bf16)
            total = jnp.sum(w.astype(f32), axis=1, keepdims=True)
            acc = jnp.dot(
                w, o_rows[:, h * head_dim:(h + 1) * head_dim], preferred_element_type=f32
            )
            safe = jnp.where(total > 0.0, total, 1.0)
            tab[j, :, h * head_dim:(h + 1) * head_dim] = (acc / safe).astype(bf16)
            lse_r = jnp.where(total > 0.0, top_r + jnp.log(safe), VERY_LOW)
            row = jnp.sum(jnp.where(lane_p == sub_p, lse_r, 0.0), axis=0, keepdims=True)
            tile = jnp.where(row8 == h, row, tile)
        tab_lse[j] = tile

    def rows_of(j, c):
        return tab.at[j, pl.ds(pl.multiple_of(c * rows, rows), rows)]

    slot = core * RING + s
    for k, same, cross in ((2, s_2, s_2_x), (1, s_up, s_up_x), (-1, s_dn, s_dn_x)):
        j = ring(s, k)
        column(j)
        send(rows_of(j, core), home.at[slot], same, 8, 22)
        send(tab_lse.at[j], home_lse.at[slot], same, 9, 23)
        send(rows_of(j, other), home.at[slot], cross, 8, 22)
        send(tab_lse.at[j], home_lse.at[slot], cross, 9, 23)
    column(s)
    send(rows_of(s, other), home.at[slot], sib, 8, 22)
    send(tab_lse.at[s], home_lse.at[slot], sib, 9, 23)
    home[slot] = tab[s, pl.ds(pl.multiple_of(core * rows, rows), rows)]
    home_lse[slot] = tab_lse[s]
    sources = 2 * RING
    wait_bytes(home_lse.at[pl.ds(0, sources - 1)], recv_sem.at[23])
    wait_bytes(home.at[pl.ds(0, sources - 1)], recv_sem.at[22])

    sub_r = lax.broadcasted_iota(jnp.int32, (rows, lane_n), 0)
    lane_r = lax.broadcasted_iota(jnp.int32, (rows, lane_n), 1)
    diag = lane_r == sub_r + core * rows
    new_value = new_kv[:, head_dim:].astype(f32)
    attention = []
    for h in range(heads):
        cols_h = [
            jnp.sum(jnp.where(diag, home_lse[n, h:h + 1, :], 0.0), axis=1, keepdims=True)
            for n in range(sources)
        ]
        top_h = own_score[h]
        for c in cols_h:
            top_h = jnp.maximum(top_h, c)
        w = jnp.exp(own_score[h] - top_h)
        mixed, denominator = w * new_value, w
        for n in range(sources):
            w = jnp.exp(cols_h[n] - top_h)
            denominator = denominator + w
            mixed = mixed + w * home[n, :, h * head_dim:(h + 1) * head_dim].astype(f32)
        attention.append((mixed / denominator).astype(bf16))
    att = jnp.concatenate(attention, axis=1)

    for k in (2, 1, 3):
        t = lax.rem(tp + k, RING)
        part[t] = jnp.dot(att, weight[t], preferred_element_type=f32).astype(bf16)
        send(part.at[t], part_in.at[tp], tps[k - 1], 10, 24)
    total = jnp.dot(att, weight[tp], preferred_element_type=f32) + residual[...].astype(f32)
    wait_bytes(part_in.at[pl.ds(0, RING - 1)], recv_sem.at[24])
    for k in range(1, RING):
        total = total + part_in[lax.rem(tp + k, RING)].astype(f32)
    out_ref[...] = total.astype(bf16)

    wait_bytes(q_rel.at[pl.ds(0, 15)], send_sem.at[0])
    order_to_sib.wait_send()
    for copy in order_copies:
        copy.wait_send()
    wait_bytes(pick_out, send_sem.at[5])
    wait_bytes(o_all.at[pl.ds(0, RING - 1)], send_sem.at[6])
    wait_bytes(lse_all.at[pl.ds(0, RING - 1)], send_sem.at[7])
    wait_bytes(home.at[pl.ds(0, sources - 1)], send_sem.at[8])
    wait_bytes(home_lse.at[pl.ds(0, sources - 1)], send_sem.at[9])
    wait_bytes(part_in.at[pl.ds(0, RING - 1)], send_sem.at[10])


def local(residual, queries, new_kv, cache, out_weight, block_counts, last_fill, block_order):
    rows, cols = residual.shape
    num_blocks, block_len, width = cache.shape
    head_dim = width // 2
    q_cols = queries.shape[1]
    requests = block_counts.shape[0]
    lanes = 128
    any_spec = pl.BlockSpec(memory_space=pl.ANY)
    f32, bf16 = jnp.float32, jnp.bfloat16
    return pl.pallas_call(
        kernel,
        out_shape=jax.ShapeDtypeStruct((rows, cols), bf16),
        in_specs=[any_spec] * 8,
        out_specs=pl.BlockSpec(memory_space=pltpu.VMEM),
        scratch_shapes=[
            pltpu.VMEM(cache.shape, bf16),
            pltpu.VMEM((RING, q_cols, cols), bf16),
            pltpu.VMEM((rows, cols), bf16),
            pltpu.VMEM((rows, width), bf16),
            pltpu.VMEM((rows, q_cols), bf16),
            pltpu.VMEM((requests // lanes, lanes), jnp.int32),
            pltpu.VMEM((requests // lanes, lanes), jnp.int32),
            pltpu.VMEM((RING, 1, num_blocks), jnp.int32),
            pltpu.VMEM((RING * RING, rows, q_cols), bf16),
            pltpu.VMEM((requests // lanes, lanes), f32),
            pltpu.VMEM((requests // lanes, lanes), f32),
            pltpu.VMEM((2, num_blocks, requests // 2), bf16),
            pltpu.VMEM((2, num_blocks, q_cols), f32),
            pltpu.VMEM((1, num_blocks), jnp.int32),
            pltpu.VMEM((GROUPS, num_blocks // GROUPS, q_cols), bf16),
            pltpu.VMEM((GROUPS, num_blocks // GROUPS, q_cols), bf16),
            pltpu.VMEM((num_blocks, 8, head_dim), f32),
            pltpu.VMEM((num_blocks, 8, block_len), f32),
            pltpu.VMEM((num_blocks, 8, head_dim), f32),
            pltpu.VMEM((RING, GROUPS, num_blocks // GROUPS, q_cols), bf16),
            pltpu.VMEM((RING, 8, lanes), f32),
            pltpu.VMEM((RING, 2 * rows, q_cols), bf16),
            pltpu.VMEM((RING, 8, lanes), f32),
            pltpu.VMEM((2 * RING, rows, q_cols), bf16),
            pltpu.VMEM((2 * RING, 8, lanes), f32),
            pltpu.VMEM((RING, rows, cols), bf16),
            pltpu.VMEM((RING, rows, cols), bf16),
            pltpu.SemaphoreType.DMA((11,)),
            pltpu.SemaphoreType.DMA((25,)),
            pltpu.SemaphoreType.DMA((GROUPS,)),
            pltpu.SemaphoreType.DMA((8,)),
        ],
        compiler_params=pltpu.CompilerParams(
            collective_id=0, has_side_effects=True, vmem_limit_bytes=60 * 1024 * 1024
        ),
    )(
        block_order.reshape(1, num_blocks),
        block_counts.reshape(requests // lanes, lanes),
        last_fill.reshape(requests // lanes, lanes),
        residual, queries, new_kv, cache, out_weight,
    )


def solution(mesh):
    in_specs = (
        P("seq", "tp"), P("seq", "tp"), P("seq", None), P("seq", None, None), P("tp", None),
        P(), P(), P("seq"),
    )
    return jax.shard_map(
        local, mesh=mesh, in_specs=in_specs, out_specs=P("seq", "tp"), check_vma=False
    )
```

```python
import jax
import jax.numpy as jnp
from jax import lax
from jax.experimental import pallas as pl
from jax.experimental.pallas import tpu as pltpu
from jax.sharding import PartitionSpec as P

MESH = pl.DeviceIdType.MESH
VERY_LOW = -1e30
RING = 4
GROUPS = 4


def kernel(
    order_hbm, counts_hbm, fill_hbm, residual_hbm, queries_hbm, new_kv_hbm, cache_hbm, weight_hbm,
    out_ref,
    cache, weight, residual, new_kv, q_own, counts, fill, order_all, q_rel, ends_ref, starts_ref,
    onehot_ref, early_ref, order_sib, pick_out, pick_in, q_blk, live, o_scr, o_all, lse_all, tab, tab_lse,
    home, home_lse, part, part_in, send_sem, recv_sem, cache_sem, local_sem,
):
    num_blocks, block_len, width = cache.shape
    head_dim = width // 2
    rows = q_own.shape[0]
    heads = q_own.shape[1] // head_dim
    cols = residual.shape[1]
    per_group = num_blocks // GROUPS
    inv_root = 1.0 / head_dim**0.5
    f32, bf16 = jnp.float32, jnp.bfloat16

    me = lax.axis_index("seq")
    tp = lax.axis_index("tp")
    core = lax.rem(me, 2)
    other = 1 - core
    chip = lax.div(me, 2)
    x = lax.div(chip, RING)
    z = lax.rem(chip, RING)
    f = x * other + z * core
    s = z * other + x * core

    def seq_of(fi, si, ci):
        xi = fi * other + si * core
        zi = si * other + fi * core
        return (xi * RING + zi) * 2 + ci

    def ring(a, k):
        return lax.rem(a + k + RING, RING)

    f_up = (seq_of(ring(f, 1), s, core), tp)
    f_dn = (seq_of(ring(f, -1), s, core), tp)
    s_up = (seq_of(f, ring(s, 1), core), tp)
    s_dn = (seq_of(f, ring(s, -1), core), tp)
    s_up_x = (seq_of(f, ring(s, 1), other), tp)
    s_dn_x = (seq_of(f, ring(s, -1), other), tp)
    f_2 = (seq_of(ring(f, 2), s, core), tp)
    s_2 = (seq_of(f, ring(s, 2), core), tp)
    s_2_x = (seq_of(f, ring(s, 2), other), tp)
    f_up_x = (seq_of(ring(f, 1), s, other), tp)
    f_dn_x = (seq_of(ring(f, -1), s, other), tp)
    f_2_x = (seq_of(ring(f, 2), s, other), tp)
    sib = (seq_of(f, s, other), tp)
    tps = [(me, lax.rem(tp + k, RING)) for k in range(1, RING)]

    barrier = pltpu.get_barrier_semaphore()
    peers = [
        f_up, f_dn, f_2, s_up, s_dn, s_2, f_up_x, f_dn_x, f_2_x, s_up_x, s_dn_x, s_2_x, sib
    ] + tps
    for peer in peers:
        pl.semaphore_signal(barrier, inc=1, device_id=peer, device_id_type=MESH)

    half = rows // 2
    early_n = (RING - 1) * RING
    axes = ((f_up, f_dn, f_2, s_up, s_dn), (s_up, s_dn, s_2, f_up, f_dn))

    def slot_of(h, i, j):
        n = (0, 2, 3, 1)[j % RING] * RING + i % RING
        return h * early_n + n if n < early_n else early_n + n + h * RING

    own_q = pltpu.make_async_copy(queries_hbm, q_own, local_sem.at[0])
    own_q.start()
    small = [
        pltpu.make_async_copy(order_hbm, order_all.at[f], local_sem.at[1]),
        pltpu.make_async_copy(counts_hbm, counts, local_sem.at[2]),
        pltpu.make_async_copy(fill_hbm, fill, local_sem.at[3]),
        pltpu.make_async_copy(new_kv_hbm, new_kv, local_sem.at[4]),
        pltpu.make_async_copy(residual_hbm, residual, local_sem.at[5]),
    ] + [
        pltpu.make_async_copy(
            queries_hbm.at[pl.ds(h * half, half)], q_rel.at[slot_of(h, 0, 0)], local_sem.at[6 + h]
        )
        for h in range(2)
    ]
    for copy in small:
        copy.start()

    cache_copies = [
        pltpu.make_async_copy(
            cache_hbm.at[pl.ds(i * per_group, per_group)],
            cache.at[pl.ds(i * per_group, per_group)],
            cache_sem.at[i],
        )
        for i in range(GROUPS)
    ]
    for copy in cache_copies:
        copy.start()
    weight_copies = [
        pltpu.make_async_copy(
            weight_hbm.at[:, pl.ds(t * cols, cols)], weight.at[t], local_sem.at[8]
        )
        for t in range(RING)
    ]
    for copy in weight_copies:
        copy.start()

    def send(src, dst, peer, ss, rs):
        copy = pltpu.make_async_remote_copy(
            src_ref=src, dst_ref=dst, send_sem=send_sem.at[ss], recv_sem=recv_sem.at[rs],
            device_id=peer, device_id_type=MESH,
        )
        copy.start()
        return copy

    def wait_bytes(ref, sem):
        pltpu.make_async_copy(ref, ref, sem).wait()

    own_q.wait()
    pl.semaphore_wait(barrier, len(peers))

    def to_b(h, i, src=None):
        b_up, b_dn = axes[h][3:]
        src = q_rel.at[slot_of(h, i, 0)] if src is None else src
        n = 11 * h + 3 + 2 * (i % RING)
        return (
            send(src, q_rel.at[slot_of(h, i, -1)], b_up, 0, n),
            send(src, q_rel.at[slot_of(h, i, 1)], b_dn, 0, n + 1),
        )

    own = [q_own.at[pl.ds(h * half, half)] for h in range(2)]
    firsts = [
        [
            send(own[h], q_rel.at[slot_of(h, i, 0)], peer, 0, 11 * h + k)
            for k, (i, peer) in enumerate(zip((-1, 1, 2), axes[h]))
        ]
        for h in range(2)
    ]
    b_copies = {(h, 0): to_b(h, 0, own[h]) for h in range(2)}

    for copy in small:
        copy.wait()
    order_own = order_all.at[f]
    order_to_sib = send(order_own, order_sib, sib, 1, 23)
    order_copies = [
        send(order_own, order_own, peer, 2 + k, 24 + k) for k, peer in enumerate((f_up, f_dn, f_2))
    ]

    counts_f = counts[...].astype(f32)
    fill_f = fill[...].astype(f32)
    lane_n = counts_f.shape[1]
    sub_i = lax.broadcasted_iota(jnp.int32, (lane_n, lane_n), 0)
    lane_i = lax.broadcasted_iota(jnp.int32, (lane_n, lane_n), 1)
    upper = (sub_i <= lane_i).astype(f32).astype(bf16)
    cum = jnp.dot(counts_f.astype(bf16), upper, preferred_element_type=f32)
    before = jnp.zeros((1, 1), f32)
    pieces = counts_f.shape[0]
    for k in range(pieces):
        ends_k = cum[k:k + 1, :] + before
        ends_ref[k:k + 1, :] = ends_k
        starts_ref[k:k + 1, :] = ends_k - counts_f[k:k + 1, :]
        before = before + jnp.sum(counts_f[k:k + 1, :], axis=1, keepdims=True)

    sub64 = lax.broadcasted_iota(jnp.int32, (num_blocks, num_blocks), 0)
    lane64 = lax.broadcasted_iota(jnp.int32, (num_blocks, num_blocks), 1)

    def column_of(order_row):
        return jnp.sum(
            jnp.where(
                sub64 == lane64, jnp.broadcast_to(order_row, (num_blocks, num_blocks)), 0.0
            ),
            axis=1, keepdims=True,
        )

    places_of = {
        slot_of(h, i, j): (h, i, j) for h in range(2) for i in range(RING) for j in range(RING)
    }
    row_lane = lax.broadcasted_iota(jnp.int32, (1, RING * rows), 1)
    row_ids = []
    for n in range(RING):
        ids = row_lane
        for k in range(2 * RING):
            h, i, j = places_of[n * 2 * RING + k]
            fi, si = (i, j) if h == 0 else (j, i)
            base = seq_of(ring(f, fi), ring(s, si), core) * rows + h * half - k * half
            here = (row_lane >= k * half) & (row_lane < (k + 1) * half)
            ids = jnp.where(here, row_lane + base, ids)
        row_ids.append(ids.astype(f32))

    def select(which, order_col):
        passed = jnp.zeros((num_blocks, lane_n), f32)
        for k in range(pieces):
            passed = passed + jnp.where(ends_ref[k:k + 1, :] <= order_col, 1.0, 0.0)
        request = jnp.sum(passed, axis=1, keepdims=True)
        for n in range(RING):
            onehot_ref[which, :, n * RING * rows:(n + 1) * RING * rows] = (
                jnp.where(row_ids[n] == request, 1.0, 0.0).astype(bf16)
            )

    order_col = column_of(order_all[f].astype(f32))
    fill_raw = jnp.zeros((num_blocks, lane_n), f32)
    for k in range(pieces):
        fill_raw = fill_raw + jnp.where(
            ends_ref[k:k + 1, :] == order_col + 1.0, fill_f[k:k + 1, :], 0.0
        )
    fill_sum = jnp.sum(fill_raw, axis=1, keepdims=True)
    live_n = jnp.where(fill_sum > 0.0, fill_sum, float(block_len))
    select(0, order_col)
    order_to_sib.wait_recv()
    select(1, column_of(order_sib[...].astype(f32)))
    for h in range(8):
        live[:, h, :] = jnp.broadcast_to(live_n, (num_blocks, block_len))
    q_blk[...] = jnp.zeros(q_blk.shape, f32)

    left, right = pl.ds(0, heads * head_dim // 2), pl.ds(heads * head_dim // 2, heads * head_dim // 2)

    def forward_b(h, i):
        b_up, b_dn = axes[h][3:]
        up, dn = b_copies[h, i]
        to = slot_of(h, i, 2)
        up.wait_recv()
        send(q_rel.at[slot_of(h, i, -1), :, left], q_rel.at[to, :, left], b_up, 0, 22)
        dn.wait_recv()
        send(q_rel.at[slot_of(h, i, 1), :, right], q_rel.at[to, :, right], b_dn, 0, 22)

    for k, i in enumerate((-1, 1, 2)):
        for h in range(2):
            firsts[h][k].wait_recv()
            b_copies[h, i] = to_b(h, i)
    for i in (0, -1, 1, 2):
        for h in range(2):
            forward_b(h, i)

    early = q_rel[0:2 * early_n].reshape(early_n * rows, heads * head_dim)
    for which in range(2):
        early_ref[which] = jnp.dot(
            onehot_ref[which, :, :early_n * rows], early, preferred_element_type=f32
        )
    wait_bytes(q_rel.at[pl.ds(0, 2 * RING)], recv_sem.at[22])
    late = q_rel[2 * early_n:].reshape(RING * rows, heads * head_dim)

    def pick(which):
        return early_ref[which] + jnp.dot(
            onehot_ref[which, :, early_n * rows:], late, preferred_element_type=f32
        )

    pick_out[...] = pick(1).astype(bf16).reshape(pick_out.shape)
    picks = [send(pick_out.at[g], pick_in.at[g], sib, 5, 27 + g) for g in range(GROUPS)]
    early_ref[0] = pick(0)

    lse_all[f] = jnp.zeros((8, lane_n), f32)
    token = lax.broadcasted_iota(jnp.int32, (8, block_len), 1).astype(f32)
    lane8 = lax.broadcasted_iota(jnp.int32, (8, lane_n), 1)

    for g in range(GROUPS):
        cache_copies[g].wait()
        picks[g].wait_recv()
        first = g * per_group
        picked = early_ref[0, first:first + per_group, :] + pick_in[g].astype(f32)
        for h in range(heads):
            q_blk[first:first + per_group, h, :] = picked[:, h * head_dim:(h + 1) * head_dim]
        blocks = range(g * per_group, (g + 1) * per_group)
        lse_rows = lse_all[f]
        scores = []
        for b in blocks:
            q8 = q_blk[b].astype(bf16)
            scores.append(
                lax.dot_general(
                    q8, cache[b, :, :head_dim], (((1,), (1,)), ((), ())), preferred_element_type=f32
                )
            )
        for b, score in zip(blocks, scores):
            alive = token < live[b]
            score = jnp.where(alive, score * inv_root, VERY_LOW)
            top_b = jnp.max(score, axis=1, keepdims=True)
            w = jnp.where(alive, jnp.exp(score - top_b), 0.0)
            total = jnp.sum(w, axis=1, keepdims=True)
            acc = jnp.dot(w.astype(bf16), cache[b, :, head_dim:], preferred_element_type=f32)
            o_scr[b] = acc / total
            lse_rows = jnp.where(lane8 == b, top_b + jnp.log(total), lse_rows)
        lse_all[f] = lse_rows
        for h in range(heads):
            o_all[f, g, :, h * head_dim:(h + 1) * head_dim] = (
                o_scr[g * per_group:(g + 1) * per_group, h, :].astype(bf16)
            )
        ref = o_all.at[f, g]
        for peer in (f_2, f_up, f_dn):
            send(ref, ref, peer, 6, 31)
    ref = lse_all.at[f]
    for peer in (f_2, f_up, f_dn):
        send(ref, ref, peer, 7, 32)

    q_f = q_own[...].astype(f32)
    new_key = new_kv[:, :head_dim].astype(f32)
    own_score = [
        jnp.sum(q_f[:, h * head_dim:(h + 1) * head_dim] * new_key, axis=1, keepdims=True) * inv_root
        for h in range(heads)
    ]
    wait_bytes(weight, local_sem.at[8])
    for copy in order_copies:
        copy.wait_recv()
    wait_bytes(lse_all.at[pl.ds(0, RING - 1)], recv_sem.at[32])
    wait_bytes(o_all.at[pl.ds(0, RING - 1)], recv_sem.at[31])

    def pair(a, b):
        lanes = lax.broadcasted_iota(jnp.int32, a.shape, 1)
        return jnp.where(lanes < num_blocks, a, pltpu.roll(b, num_blocks, 1))

    lse = jnp.concatenate(
        [pair(lse_all[0], lse_all[1]), pair(lse_all[2], lse_all[3])], axis=1
    )

    def order_pair(a, b):
        return jnp.concatenate([order_all[a].astype(f32), order_all[b].astype(f32)], axis=1)

    order_lanes = jnp.concatenate([order_pair(0, 1), order_pair(2, 3)], axis=1)
    o_rows = o_all[...].reshape(RING * num_blocks, heads * head_dim)
    places = 2 * rows
    sub_p = lax.broadcasted_iota(jnp.int32, (places, lane_n), 0)
    lane_p = lax.broadcasted_iota(jnp.int32, (places, lane_n), 1)
    row8 = lax.broadcasted_iota(jnp.int32, (8, lane_n), 0)

    def column(j):
        first = (RING * places * f + places * j) * other + (RING * places * j + places * f) * core
        piece = lax.div(first, lane_n)
        offset = lax.rem(first, lane_n)
        diag = lane_p == sub_p + offset
        end = jnp.sum(jnp.where(diag, ends_ref[pl.ds(piece, 1), :], 0.0), axis=1, keepdims=True)
        start = jnp.sum(jnp.where(diag, starts_ref[pl.ds(piece, 1), :], 0.0), axis=1, keepdims=True)
        member = (start <= order_lanes) & (order_lanes < end)
        tile = jnp.zeros((8, lane_n), f32)
        for h in range(heads):
            here = jnp.where(member, lse[h:h + 1, :], VERY_LOW)
            top_r = jnp.max(here, axis=1, keepdims=True)
            w = jnp.where(member, jnp.exp(here - top_r), 0.0).astype(bf16)
            total = jnp.sum(w.astype(f32), axis=1, keepdims=True)
            acc = jnp.dot(
                w, o_rows[:, h * head_dim:(h + 1) * head_dim], preferred_element_type=f32
            )
            safe = jnp.where(total > 0.0, total, 1.0)
            tab[j, :, h * head_dim:(h + 1) * head_dim] = (acc / safe).astype(bf16)
            lse_r = jnp.where(total > 0.0, top_r + jnp.log(safe), VERY_LOW)
            row = jnp.sum(jnp.where(lane_p == sub_p, lse_r, 0.0), axis=0, keepdims=True)
            tile = jnp.where(row8 == h, row, tile)
        tab_lse[j] = tile

    def rows_of(j, c):
        return tab.at[j, pl.ds(pl.multiple_of(c * rows, rows), rows)]

    slot = core * RING + s
    for k, same, cross in ((2, s_2, s_2_x), (1, s_up, s_up_x), (-1, s_dn, s_dn_x)):
        j = ring(s, k)
        column(j)
        send(rows_of(j, core), home.at[slot], same, 8, 33)
        send(tab_lse.at[j], home_lse.at[slot], same, 9, 34)
        send(rows_of(j, other), home.at[slot], cross, 8, 33)
        send(tab_lse.at[j], home_lse.at[slot], cross, 9, 34)
    column(s)
    send(rows_of(s, other), home.at[slot], sib, 8, 33)
    send(tab_lse.at[s], home_lse.at[slot], sib, 9, 34)
    home[slot] = tab[s, pl.ds(pl.multiple_of(core * rows, rows), rows)]
    home_lse[slot] = tab_lse[s]
    sources = 2 * RING
    wait_bytes(home_lse.at[pl.ds(0, sources - 1)], recv_sem.at[34])
    wait_bytes(home.at[pl.ds(0, sources - 1)], recv_sem.at[33])

    sub_r = lax.broadcasted_iota(jnp.int32, (rows, lane_n), 0)
    lane_r = lax.broadcasted_iota(jnp.int32, (rows, lane_n), 1)
    diag = lane_r == sub_r + core * rows
    new_value = new_kv[:, head_dim:].astype(f32)
    attention = []
    for h in range(heads):
        cols_h = [
            jnp.sum(jnp.where(diag, home_lse[n, h:h + 1, :], 0.0), axis=1, keepdims=True)
            for n in range(sources)
        ]
        top_h = own_score[h]
        for c in cols_h:
            top_h = jnp.maximum(top_h, c)
        w = jnp.exp(own_score[h] - top_h)
        mixed, denominator = w * new_value, w
        for n in range(sources):
            w = jnp.exp(cols_h[n] - top_h)
            denominator = denominator + w
            mixed = mixed + w * home[n, :, h * head_dim:(h + 1) * head_dim].astype(f32)
        attention.append((mixed / denominator).astype(bf16))
    att = jnp.concatenate(attention, axis=1)

    for k in (2, 1, 3):
        t = lax.rem(tp + k, RING)
        part[t] = jnp.dot(att, weight[t], preferred_element_type=f32).astype(bf16)
        send(part.at[t], part_in.at[tp], tps[k - 1], 10, 35)
    total = jnp.dot(att, weight[tp], preferred_element_type=f32) + residual[...].astype(f32)
    wait_bytes(part_in.at[pl.ds(0, RING - 1)], recv_sem.at[35])
    for k in range(1, RING):
        total = total + part_in[lax.rem(tp + k, RING)].astype(f32)
    out_ref[...] = total.astype(bf16)

    wait_bytes(q_rel.at[pl.ds(0, 30)], send_sem.at[0])
    order_to_sib.wait_send()
    for copy in order_copies:
        copy.wait_send()
    wait_bytes(pick_out, send_sem.at[5])
    wait_bytes(o_all.at[pl.ds(0, RING - 1)], send_sem.at[6])
    wait_bytes(lse_all.at[pl.ds(0, RING - 1)], send_sem.at[7])
    wait_bytes(home.at[pl.ds(0, sources - 1)], send_sem.at[8])
    wait_bytes(home_lse.at[pl.ds(0, sources - 1)], send_sem.at[9])
    wait_bytes(part_in.at[pl.ds(0, RING - 1)], send_sem.at[10])


def local(residual, queries, new_kv, cache, out_weight, block_counts, last_fill, block_order):
    rows, cols = residual.shape
    num_blocks, block_len, width = cache.shape
    head_dim = width // 2
    q_cols = queries.shape[1]
    requests = block_counts.shape[0]
    lanes = 128
    any_spec = pl.BlockSpec(memory_space=pl.ANY)
    f32, bf16 = jnp.float32, jnp.bfloat16
    return pl.pallas_call(
        kernel,
        out_shape=jax.ShapeDtypeStruct((rows, cols), bf16),
        in_specs=[any_spec] * 8,
        out_specs=pl.BlockSpec(memory_space=pltpu.VMEM),
        scratch_shapes=[
            pltpu.VMEM(cache.shape, bf16),
            pltpu.VMEM((RING, q_cols, cols), bf16),
            pltpu.VMEM((rows, cols), bf16),
            pltpu.VMEM((rows, width), bf16),
            pltpu.VMEM((rows, q_cols), bf16),
            pltpu.VMEM((requests // lanes, lanes), jnp.int32),
            pltpu.VMEM((requests // lanes, lanes), jnp.int32),
            pltpu.VMEM((RING, 1, num_blocks), jnp.int32),
            pltpu.VMEM((2 * RING * RING, rows // 2, q_cols), bf16),
            pltpu.VMEM((requests // lanes, lanes), f32),
            pltpu.VMEM((requests // lanes, lanes), f32),
            pltpu.VMEM((2, num_blocks, requests // 2), bf16),
            pltpu.VMEM((2, num_blocks, q_cols), f32),
            pltpu.VMEM((1, num_blocks), jnp.int32),
            pltpu.VMEM((GROUPS, num_blocks // GROUPS, q_cols), bf16),
            pltpu.VMEM((GROUPS, num_blocks // GROUPS, q_cols), bf16),
            pltpu.VMEM((num_blocks, 8, head_dim), f32),
            pltpu.VMEM((num_blocks, 8, block_len), f32),
            pltpu.VMEM((num_blocks, 8, head_dim), f32),
            pltpu.VMEM((RING, GROUPS, num_blocks // GROUPS, q_cols), bf16),
            pltpu.VMEM((RING, 8, lanes), f32),
            pltpu.VMEM((RING, 2 * rows, q_cols), bf16),
            pltpu.VMEM((RING, 8, lanes), f32),
            pltpu.VMEM((2 * RING, rows, q_cols), bf16),
            pltpu.VMEM((2 * RING, 8, lanes), f32),
            pltpu.VMEM((RING, rows, cols), bf16),
            pltpu.VMEM((RING, rows, cols), bf16),
            pltpu.SemaphoreType.DMA((11,)),
            pltpu.SemaphoreType.DMA((36,)),
            pltpu.SemaphoreType.DMA((GROUPS,)),
            pltpu.SemaphoreType.DMA((9,)),
        ],
        compiler_params=pltpu.CompilerParams(
            collective_id=0, has_side_effects=True, vmem_limit_bytes=60 * 1024 * 1024
        ),
    )(
        block_order.reshape(1, num_blocks),
        block_counts.reshape(requests // lanes, lanes),
        last_fill.reshape(requests // lanes, lanes),
        residual, queries, new_kv, cache, out_weight,
    )


def solution(mesh):
    in_specs = (
        P("seq", "tp"), P("seq", "tp"), P("seq", None), P("seq", None, None), P("tp", None),
        P(), P(), P("seq"),
    )
    return jax.shard_map(
        local, mesh=mesh, in_specs=in_specs, out_specs=P("seq", "tp"), check_vma=False
    )
```

```python
import jax
import jax.numpy as jnp
from jax import lax
from jax.experimental import pallas as pl
from jax.experimental.pallas import tpu as pltpu
from jax.sharding import PartitionSpec as P

MESH = pl.DeviceIdType.MESH
VERY_LOW = -1e30
RING = 4
GROUPS = 4


def kernel(
    order_hbm, counts_hbm, fill_hbm, residual_hbm, queries_hbm, new_kv_hbm, cache_hbm, weight_hbm,
    out_ref,
    cache, weight, residual, new_kv, q_own, counts, fill, order_all, q_rel, ends_ref, starts_ref,
    onehot_ref, early_ref, order_sib, pick_out, pick_in, q_blk, live, o_scr, o_all, lse_all, tab, tab_lse,
    home, home_lse, part, part_in, send_sem, recv_sem, cache_sem, local_sem,
):
    num_blocks, block_len, width = cache.shape
    head_dim = width // 2
    rows = q_own.shape[0]
    heads = q_own.shape[1] // head_dim
    cols = residual.shape[1]
    per_group = num_blocks // GROUPS
    inv_root = 1.0 / head_dim**0.5
    f32, bf16 = jnp.float32, jnp.bfloat16

    me = lax.axis_index("seq")
    tp = lax.axis_index("tp")
    core = lax.rem(me, 2)
    other = 1 - core
    chip = lax.div(me, 2)
    x = lax.div(chip, RING)
    z = lax.rem(chip, RING)
    f = x * other + z * core
    s = z * other + x * core

    def seq_of(fi, si, ci):
        xi = fi * other + si * core
        zi = si * other + fi * core
        return (xi * RING + zi) * 2 + ci

    def ring(a, k):
        return lax.rem(a + k + RING, RING)

    f_up = (seq_of(ring(f, 1), s, core), tp)
    f_dn = (seq_of(ring(f, -1), s, core), tp)
    s_up = (seq_of(f, ring(s, 1), core), tp)
    s_dn = (seq_of(f, ring(s, -1), core), tp)
    s_up_x = (seq_of(f, ring(s, 1), other), tp)
    s_dn_x = (seq_of(f, ring(s, -1), other), tp)
    f_2 = (seq_of(ring(f, 2), s, core), tp)
    s_2 = (seq_of(f, ring(s, 2), core), tp)
    s_2_x = (seq_of(f, ring(s, 2), other), tp)
    f_up_x = (seq_of(ring(f, 1), s, other), tp)
    f_dn_x = (seq_of(ring(f, -1), s, other), tp)
    f_2_x = (seq_of(ring(f, 2), s, other), tp)
    sib = (seq_of(f, s, other), tp)
    tps = [(me, lax.rem(tp + k, RING)) for k in range(1, RING)]

    barrier = pltpu.get_barrier_semaphore()
    peers = [
        f_up, f_dn, f_2, s_up, s_dn, s_2, f_up_x, f_dn_x, f_2_x, s_up_x, s_dn_x, s_2_x, sib
    ] + tps
    for peer in peers:
        pl.semaphore_signal(barrier, inc=1, device_id=peer, device_id_type=MESH)

    half = rows // 2
    early_n = (RING - 1) * RING
    axes = ((f_up, f_dn, f_2, s_up, s_dn), (s_up, s_dn, s_2, f_up, f_dn))

    def slot_of(h, i, j):
        n = (0, 2, 3, 1)[j % RING] * RING + i % RING
        return h * early_n + n if n < early_n else early_n + n + h * RING

    own_q = pltpu.make_async_copy(queries_hbm, q_own, local_sem.at[0])
    own_q.start()
    small = [
        pltpu.make_async_copy(order_hbm, order_all.at[f], local_sem.at[1]),
        pltpu.make_async_copy(counts_hbm, counts, local_sem.at[2]),
        pltpu.make_async_copy(fill_hbm, fill, local_sem.at[3]),
        pltpu.make_async_copy(new_kv_hbm, new_kv, local_sem.at[4]),
        pltpu.make_async_copy(residual_hbm, residual, local_sem.at[5]),
    ] + [
        pltpu.make_async_copy(
            queries_hbm.at[pl.ds(h * half, half)], q_rel.at[slot_of(h, 0, 0)], local_sem.at[6 + h]
        )
        for h in range(2)
    ]
    for copy in small:
        copy.start()

    cache_copies = [
        pltpu.make_async_copy(
            cache_hbm.at[pl.ds(i * per_group, per_group)],
            cache.at[pl.ds(i * per_group, per_group)],
            cache_sem.at[i],
        )
        for i in range(GROUPS)
    ]
    for copy in cache_copies:
        copy.start()
    weight_copies = [
        pltpu.make_async_copy(
            weight_hbm.at[:, pl.ds(t * cols, cols)], weight.at[t], local_sem.at[8]
        )
        for t in range(RING)
    ]
    for copy in weight_copies:
        copy.start()

    def send(src, dst, peer, ss, rs):
        copy = pltpu.make_async_remote_copy(
            src_ref=src, dst_ref=dst, send_sem=send_sem.at[ss], recv_sem=recv_sem.at[rs],
            device_id=peer, device_id_type=MESH,
        )
        copy.start()
        return copy

    def wait_bytes(ref, sem):
        pltpu.make_async_copy(ref, ref, sem).wait()

    own_q.wait()
    pl.semaphore_wait(barrier, len(peers))

    def to_b(h, i, src=None):
        b_up, b_dn = axes[h][3:]
        src = q_rel.at[slot_of(h, i, 0)] if src is None else src
        n = 11 * h + 3 + 2 * (i % RING)
        return (
            send(src, q_rel.at[slot_of(h, i, -1)], b_up, 0, n),
            send(src, q_rel.at[slot_of(h, i, 1)], b_dn, 0, n + 1),
        )

    own = [q_own.at[pl.ds(h * half, half)] for h in range(2)]
    firsts = [
        [
            send(own[h], q_rel.at[slot_of(h, i, 0)], peer, 0, 11 * h + k)
            for k, (i, peer) in enumerate(zip((2, -1, 1), (axes[h][2], axes[h][0], axes[h][1])))
        ]
        for h in range(2)
    ]
    b_copies = {(h, 0): to_b(h, 0, own[h]) for h in range(2)}

    for copy in small:
        copy.wait()
    order_own = order_all.at[f]
    order_to_sib = send(order_own, order_sib, sib, 1, 23)
    order_copies = [
        send(order_own, order_own, peer, 2 + k, 24 + k) for k, peer in enumerate((f_up, f_dn, f_2))
    ]

    counts_f = counts[...].astype(f32)
    fill_f = fill[...].astype(f32)
    lane_n = counts_f.shape[1]
    sub_i = lax.broadcasted_iota(jnp.int32, (lane_n, lane_n), 0)
    lane_i = lax.broadcasted_iota(jnp.int32, (lane_n, lane_n), 1)
    upper = (sub_i <= lane_i).astype(f32).astype(bf16)
    cum = jnp.dot(counts_f.astype(bf16), upper, preferred_element_type=f32)
    before = jnp.zeros((1, 1), f32)
    pieces = counts_f.shape[0]
    for k in range(pieces):
        ends_k = cum[k:k + 1, :] + before
        ends_ref[k:k + 1, :] = ends_k
        starts_ref[k:k + 1, :] = ends_k - counts_f[k:k + 1, :]
        before = before + jnp.sum(counts_f[k:k + 1, :], axis=1, keepdims=True)

    sub64 = lax.broadcasted_iota(jnp.int32, (num_blocks, num_blocks), 0)
    lane64 = lax.broadcasted_iota(jnp.int32, (num_blocks, num_blocks), 1)

    def column_of(order_row):
        return jnp.sum(
            jnp.where(
                sub64 == lane64, jnp.broadcast_to(order_row, (num_blocks, num_blocks)), 0.0
            ),
            axis=1, keepdims=True,
        )

    places_of = {
        slot_of(h, i, j): (h, i, j) for h in range(2) for i in range(RING) for j in range(RING)
    }
    row_lane = lax.broadcasted_iota(jnp.int32, (1, RING * rows), 1)
    row_ids = []
    for n in range(RING):
        ids = row_lane
        for k in range(2 * RING):
            h, i, j = places_of[n * 2 * RING + k]
            fi, si = (i, j) if h == 0 else (j, i)
            base = seq_of(ring(f, fi), ring(s, si), core) * rows + h * half - k * half
            here = (row_lane >= k * half) & (row_lane < (k + 1) * half)
            ids = jnp.where(here, row_lane + base, ids)
        row_ids.append(ids.astype(f32))

    def select(which, order_col):
        passed = jnp.zeros((num_blocks, lane_n), f32)
        for k in range(pieces):
            passed = passed + jnp.where(ends_ref[k:k + 1, :] <= order_col, 1.0, 0.0)
        request = jnp.sum(passed, axis=1, keepdims=True)
        for n in range(RING):
            onehot_ref[which, :, n * RING * rows:(n + 1) * RING * rows] = (
                jnp.where(row_ids[n] == request, 1.0, 0.0).astype(bf16)
            )

    order_col = column_of(order_all[f].astype(f32))
    fill_raw = jnp.zeros((num_blocks, lane_n), f32)
    for k in range(pieces):
        fill_raw = fill_raw + jnp.where(
            ends_ref[k:k + 1, :] == order_col + 1.0, fill_f[k:k + 1, :], 0.0
        )
    fill_sum = jnp.sum(fill_raw, axis=1, keepdims=True)
    live_n = jnp.where(fill_sum > 0.0, fill_sum, float(block_len))
    select(0, order_col)
    order_to_sib.wait_recv()
    select(1, column_of(order_sib[...].astype(f32)))
    for h in range(8):
        live[:, h, :] = jnp.broadcast_to(live_n, (num_blocks, block_len))
    q_blk[...] = jnp.zeros(q_blk.shape, f32)

    left, right = pl.ds(0, heads * head_dim // 2), pl.ds(heads * head_dim // 2, heads * head_dim // 2)

    def forward_b(h, i):
        b_up, b_dn = axes[h][3:]
        up, dn = b_copies[h, i]
        to = slot_of(h, i, 2)
        up.wait_recv()
        send(q_rel.at[slot_of(h, i, -1), :, left], q_rel.at[to, :, left], b_up, 0, 22)
        dn.wait_recv()
        send(q_rel.at[slot_of(h, i, 1), :, right], q_rel.at[to, :, right], b_dn, 0, 22)

    for k, i in ((1, -1), (2, 1), (0, 2)):
        for h in range(2):
            firsts[h][k].wait_recv()
            b_copies[h, i] = to_b(h, i)
    for i in (0, -1, 1, 2):
        for h in range(2):
            forward_b(h, i)

    early = q_rel[0:2 * early_n].reshape(early_n * rows, heads * head_dim)
    for which in range(2):
        early_ref[which] = jnp.dot(
            onehot_ref[which, :, :early_n * rows], early, preferred_element_type=f32
        )
    wait_bytes(q_rel.at[pl.ds(0, 2 * RING)], recv_sem.at[22])
    late = q_rel[2 * early_n:].reshape(RING * rows, heads * head_dim)

    def pick(which):
        return early_ref[which] + jnp.dot(
            onehot_ref[which, :, early_n * rows:], late, preferred_element_type=f32
        )

    pick_out[...] = pick(1).astype(bf16).reshape(pick_out.shape)
    picks = [send(pick_out.at[g], pick_in.at[g], sib, 5, 27 + g) for g in range(GROUPS)]
    early_ref[0] = pick(0)

    lse_all[f] = jnp.zeros((8, lane_n), f32)
    token = lax.broadcasted_iota(jnp.int32, (8, block_len), 1).astype(f32)
    lane8 = lax.broadcasted_iota(jnp.int32, (8, lane_n), 1)

    for g in range(GROUPS):
        cache_copies[g].wait()
        picks[g].wait_recv()
        first = g * per_group
        picked = early_ref[0, first:first + per_group, :] + pick_in[g].astype(f32)
        for h in range(heads):
            q_blk[first:first + per_group, h, :] = picked[:, h * head_dim:(h + 1) * head_dim]
        blocks = range(g * per_group, (g + 1) * per_group)
        lse_rows = lse_all[f]
        scores = []
        for b in blocks:
            q8 = q_blk[b].astype(bf16)
            scores.append(
                lax.dot_general(
                    q8, cache[b, :, :head_dim], (((1,), (1,)), ((), ())), preferred_element_type=f32
                )
            )
        for b, score in zip(blocks, scores):
            alive = token < live[b]
            score = jnp.where(alive, score * inv_root, VERY_LOW)
            top_b = jnp.max(score, axis=1, keepdims=True)
            w = jnp.where(alive, jnp.exp(score - top_b), 0.0)
            total = jnp.sum(w, axis=1, keepdims=True)
            acc = jnp.dot(w.astype(bf16), cache[b, :, head_dim:], preferred_element_type=f32)
            o_scr[b] = acc / total
            lse_rows = jnp.where(lane8 == b, top_b + jnp.log(total), lse_rows)
        lse_all[f] = lse_rows
        for h in range(heads):
            o_all[f, g, :, h * head_dim:(h + 1) * head_dim] = (
                o_scr[g * per_group:(g + 1) * per_group, h, :].astype(bf16)
            )
        ref = o_all.at[f, g]
        for peer in (f_2, f_up, f_dn):
            send(ref, ref, peer, 6, 31)
    ref = lse_all.at[f]
    for peer in (f_2, f_up, f_dn):
        send(ref, ref, peer, 7, 32)

    q_f = q_own[...].astype(f32)
    new_key = new_kv[:, :head_dim].astype(f32)
    own_score = [
        jnp.sum(q_f[:, h * head_dim:(h + 1) * head_dim] * new_key, axis=1, keepdims=True) * inv_root
        for h in range(heads)
    ]
    wait_bytes(weight, local_sem.at[8])
    for copy in order_copies:
        copy.wait_recv()
    wait_bytes(lse_all.at[pl.ds(0, RING - 1)], recv_sem.at[32])
    wait_bytes(o_all.at[pl.ds(0, RING - 1)], recv_sem.at[31])

    def pair(a, b):
        lanes = lax.broadcasted_iota(jnp.int32, a.shape, 1)
        return jnp.where(lanes < num_blocks, a, pltpu.roll(b, num_blocks, 1))

    lse = jnp.concatenate(
        [pair(lse_all[0], lse_all[1]), pair(lse_all[2], lse_all[3])], axis=1
    )

    def order_pair(a, b):
        return jnp.concatenate([order_all[a].astype(f32), order_all[b].astype(f32)], axis=1)

    order_lanes = jnp.concatenate([order_pair(0, 1), order_pair(2, 3)], axis=1)
    o_rows = o_all[...].reshape(RING * num_blocks, heads * head_dim)
    places = 2 * rows
    sub_p = lax.broadcasted_iota(jnp.int32, (places, lane_n), 0)
    lane_p = lax.broadcasted_iota(jnp.int32, (places, lane_n), 1)
    row8 = lax.broadcasted_iota(jnp.int32, (8, lane_n), 0)

    def column(j):
        first = (RING * places * f + places * j) * other + (RING * places * j + places * f) * core
        piece = lax.div(first, lane_n)
        offset = lax.rem(first, lane_n)
        diag = lane_p == sub_p + offset
        end = jnp.sum(jnp.where(diag, ends_ref[pl.ds(piece, 1), :], 0.0), axis=1, keepdims=True)
        start = jnp.sum(jnp.where(diag, starts_ref[pl.ds(piece, 1), :], 0.0), axis=1, keepdims=True)
        member = (start <= order_lanes) & (order_lanes < end)
        tile = jnp.zeros((8, lane_n), f32)
        for h in range(heads):
            here = jnp.where(member, lse[h:h + 1, :], VERY_LOW)
            top_r = jnp.max(here, axis=1, keepdims=True)
            w = jnp.where(member, jnp.exp(here - top_r), 0.0).astype(bf16)
            total = jnp.sum(w.astype(f32), axis=1, keepdims=True)
            acc = jnp.dot(
                w, o_rows[:, h * head_dim:(h + 1) * head_dim], preferred_element_type=f32
            )
            safe = jnp.where(total > 0.0, total, 1.0)
            tab[j, :, h * head_dim:(h + 1) * head_dim] = (acc / safe).astype(bf16)
            lse_r = jnp.where(total > 0.0, top_r + jnp.log(safe), VERY_LOW)
            row = jnp.sum(jnp.where(lane_p == sub_p, lse_r, 0.0), axis=0, keepdims=True)
            tile = jnp.where(row8 == h, row, tile)
        tab_lse[j] = tile

    def rows_of(j, c):
        return tab.at[j, pl.ds(pl.multiple_of(c * rows, rows), rows)]

    slot = core * RING + s
    for k, same, cross in ((2, s_2, s_2_x), (1, s_up, s_up_x), (-1, s_dn, s_dn_x)):
        j = ring(s, k)
        column(j)
        send(rows_of(j, core), home.at[slot], same, 8, 33)
        send(tab_lse.at[j], home_lse.at[slot], same, 9, 34)
        send(rows_of(j, other), home.at[slot], cross, 8, 33)
        send(tab_lse.at[j], home_lse.at[slot], cross, 9, 34)
    column(s)
    send(rows_of(s, other), home.at[slot], sib, 8, 33)
    send(tab_lse.at[s], home_lse.at[slot], sib, 9, 34)
    home[slot] = tab[s, pl.ds(pl.multiple_of(core * rows, rows), rows)]
    home_lse[slot] = tab_lse[s]
    sources = 2 * RING
    wait_bytes(home_lse.at[pl.ds(0, sources - 1)], recv_sem.at[34])
    wait_bytes(home.at[pl.ds(0, sources - 1)], recv_sem.at[33])

    sub_r = lax.broadcasted_iota(jnp.int32, (rows, lane_n), 0)
    lane_r = lax.broadcasted_iota(jnp.int32, (rows, lane_n), 1)
    diag = lane_r == sub_r + core * rows
    new_value = new_kv[:, head_dim:].astype(f32)
    attention = []
    for h in range(heads):
        cols_h = [
            jnp.sum(jnp.where(diag, home_lse[n, h:h + 1, :], 0.0), axis=1, keepdims=True)
            for n in range(sources)
        ]
        top_h = own_score[h]
        for c in cols_h:
            top_h = jnp.maximum(top_h, c)
        w = jnp.exp(own_score[h] - top_h)
        mixed, denominator = w * new_value, w
        for n in range(sources):
            w = jnp.exp(cols_h[n] - top_h)
            denominator = denominator + w
            mixed = mixed + w * home[n, :, h * head_dim:(h + 1) * head_dim].astype(f32)
        attention.append((mixed / denominator).astype(bf16))
    att = jnp.concatenate(attention, axis=1)

    for k in (2, 1, 3):
        t = lax.rem(tp + k, RING)
        part[t] = jnp.dot(att, weight[t], preferred_element_type=f32).astype(bf16)
        send(part.at[t], part_in.at[tp], tps[k - 1], 10, 35)
    total = jnp.dot(att, weight[tp], preferred_element_type=f32) + residual[...].astype(f32)
    wait_bytes(part_in.at[pl.ds(0, RING - 1)], recv_sem.at[35])
    for k in range(1, RING):
        total = total + part_in[lax.rem(tp + k, RING)].astype(f32)
    out_ref[...] = total.astype(bf16)

    wait_bytes(q_rel.at[pl.ds(0, 30)], send_sem.at[0])
    order_to_sib.wait_send()
    for copy in order_copies:
        copy.wait_send()
    wait_bytes(pick_out, send_sem.at[5])
    wait_bytes(o_all.at[pl.ds(0, RING - 1)], send_sem.at[6])
    wait_bytes(lse_all.at[pl.ds(0, RING - 1)], send_sem.at[7])
    wait_bytes(home.at[pl.ds(0, sources - 1)], send_sem.at[8])
    wait_bytes(home_lse.at[pl.ds(0, sources - 1)], send_sem.at[9])
    wait_bytes(part_in.at[pl.ds(0, RING - 1)], send_sem.at[10])


def local(residual, queries, new_kv, cache, out_weight, block_counts, last_fill, block_order):
    rows, cols = residual.shape
    num_blocks, block_len, width = cache.shape
    head_dim = width // 2
    q_cols = queries.shape[1]
    requests = block_counts.shape[0]
    lanes = 128
    any_spec = pl.BlockSpec(memory_space=pl.ANY)
    f32, bf16 = jnp.float32, jnp.bfloat16
    return pl.pallas_call(
        kernel,
        out_shape=jax.ShapeDtypeStruct((rows, cols), bf16),
        in_specs=[any_spec] * 8,
        out_specs=pl.BlockSpec(memory_space=pltpu.VMEM),
        scratch_shapes=[
            pltpu.VMEM(cache.shape, bf16),
            pltpu.VMEM((RING, q_cols, cols), bf16),
            pltpu.VMEM((rows, cols), bf16),
            pltpu.VMEM((rows, width), bf16),
            pltpu.VMEM((rows, q_cols), bf16),
            pltpu.VMEM((requests // lanes, lanes), jnp.int32),
            pltpu.VMEM((requests // lanes, lanes), jnp.int32),
            pltpu.VMEM((RING, 1, num_blocks), jnp.int32),
            pltpu.VMEM((2 * RING * RING, rows // 2, q_cols), bf16),
            pltpu.VMEM((requests // lanes, lanes), f32),
            pltpu.VMEM((requests // lanes, lanes), f32),
            pltpu.VMEM((2, num_blocks, requests // 2), bf16),
            pltpu.VMEM((2, num_blocks, q_cols), f32),
            pltpu.VMEM((1, num_blocks), jnp.int32),
            pltpu.VMEM((GROUPS, num_blocks // GROUPS, q_cols), bf16),
            pltpu.VMEM((GROUPS, num_blocks // GROUPS, q_cols), bf16),
            pltpu.VMEM((num_blocks, 8, head_dim), f32),
            pltpu.VMEM((num_blocks, 8, block_len), f32),
            pltpu.VMEM((num_blocks, 8, head_dim), f32),
            pltpu.VMEM((RING, GROUPS, num_blocks // GROUPS, q_cols), bf16),
            pltpu.VMEM((RING, 8, lanes), f32),
            pltpu.VMEM((RING, 2 * rows, q_cols), bf16),
            pltpu.VMEM((RING, 8, lanes), f32),
            pltpu.VMEM((2 * RING, rows, q_cols), bf16),
            pltpu.VMEM((2 * RING, 8, lanes), f32),
            pltpu.VMEM((RING, rows, cols), bf16),
            pltpu.VMEM((RING, rows, cols), bf16),
            pltpu.SemaphoreType.DMA((11,)),
            pltpu.SemaphoreType.DMA((36,)),
            pltpu.SemaphoreType.DMA((GROUPS,)),
            pltpu.SemaphoreType.DMA((9,)),
        ],
        compiler_params=pltpu.CompilerParams(
            collective_id=0, has_side_effects=True, vmem_limit_bytes=60 * 1024 * 1024
        ),
    )(
        block_order.reshape(1, num_blocks),
        block_counts.reshape(requests // lanes, lanes),
        last_fill.reshape(requests // lanes, lanes),
        residual, queries, new_kv, cache, out_weight,
    )


def solution(mesh):
    in_specs = (
        P("seq", "tp"), P("seq", "tp"), P("seq", None), P("seq", None, None), P("tp", None),
        P(), P(), P("seq"),
    )
    return jax.shard_map(
        local, mesh=mesh, in_specs=in_specs, out_specs=P("seq", "tp"), check_vma=False
    )
```
